32 devices in a mesh: groups: 2 (over y), rows: 4 (over z), cols: 4 (over x, core).
Axes of the slice: x: 2, y: 2, z: 4, core: 2. Of those that a mesh axis runs over, the one named last changes fastest.
Arguments:
- tokens: bfloat16 [112, 112, 256], P(('groups', 'rows'), 'cols'), parts along dimension 0, may hold values from -6 to 6
- cotangent: bfloat16 [56, 56, 512], P(('groups', 'rows'), 'cols'), parts along dimension 0, may hold values from -6 to 6
- shift_offsets: int32 [4], replicated, may hold values from 1 to 6
- norm2_gain: float32 [256], replicated, may hold values from 0.1 to 1.9
- qkv2: bfloat16 [256, 768], replicated, may hold values from -0.375 to 0.375
- proj2: bfloat16 [256, 256], replicated, may hold values from -0.375 to 0.375
- merge_gain: float32 [1024], replicated, may hold values from 0.1 to 1.9
- merge_weight: bfloat16 [1024, 512], replicated, may hold values from -0.1875 to 0.1875
- norm3_gain: float32 [512], replicated, may hold values from 0.1 to 1.9
- qkv3: bfloat16 [512, 1536], replicated, may hold values from -0.25 to 0.25
- proj3: bfloat16 [512, 512], replicated, may hold values from -0.25 to 0.25
Outputs:
- merged_out: bfloat16 [56, 56, 512], P(('groups', 'rows'), 'cols'), parts along dimension 0
- tokens_grad: bfloat16 [112, 112, 256], P(('groups', 'rows'), 'cols'), parts along dimension 0
- gain_grads: float32 [3584], P('groups'), parts along dimension 0
- qkv2_grad: bfloat16 [393216], P(('groups', 'rows', 'cols')), parts along dimension 0
- proj2_grad: bfloat16 [131072], P(('groups', 'rows', 'cols')), parts along dimension 0
- merge_grad: bfloat16 [1048576], P(('groups', 'rows', 'cols')), parts along dimension 0
- qkv3_grad: bfloat16 [1572864], P(('groups', 'rows', 'cols')), parts along dimension 0
- proj3_grad: bfloat16 [524288], P(('groups', 'rows', 'cols')), parts along dimension 0
The draws below stay inside these ranges and needn't reach their ends.
There are 2 independent parts, one for each index of `groups`. The reference program is written for one: setup_inputs(seed, part) draws one part's arguments, and reference() takes and returns one part's arrays. A program takes and returns all parts, laid end to end along the dimension named above; an argument that names none is the same for every part. Nothing has to cross between parts.
All inputs are finite; a program needn't handle non-finite values.
Results may differ from the reference program's by a relative error of at most 0.033.
Values may be sent and summed in bfloat16 or wider, within the bound.
A program may use at most 128 MiB of HBM per device.

```python
import jax
import jax.numpy as jnp
from jax import lax

C2 = 256
C3 = 512
HEADS2 = 8
HEADS3 = 16
WIN = 7
H2 = 56
W2 = 112


def plant(array, key, smallest, top_value):
    extent = array.shape
    place = [jax.random.randint(jax.random.fold_in(key, axis), (), 0, extent[axis]) for axis in range(len(extent))]
    array = array.at[tuple(place)].set(smallest)
    longest = extent.index(max(extent))
    place[longest] = (place[longest] + 1) % extent[longest]
    return array.at[tuple(place)].set(top_value)


def shard_levels(own_key, shape, split, least, top_value):
    level = 1.0
    for dim, parts in split:
        heights = jax.random.uniform(jax.random.fold_in(jax.random.fold_in(own_key, 6), dim), (parts,), jnp.float32, least / len(split), top_value / len(split))
        level = level * jnp.repeat(jnp.exp(heights), shape[dim] // parts).reshape((-1,) + (1,) * (len(shape) - 1 - dim))
    return level


def noise(rng, extent, scale, bound, pieces=(), kind=jnp.bfloat16):
    result = jax.random.normal(rng, extent, jnp.float32) * scale
    if len(pieces) > 0:
        result = shard_levels(rng, extent, pieces, -0.22, 0.18) * result
    return jnp.clip(result, min=-bound, max=bound).astype(kind)


def setup_inputs(seed: int = 0, part: int = 0) -> dict:
    splits = jax.random.split(jax.random.key(seed), 12)
    part_splits = jax.random.split(jax.random.fold_in(splits[11], part), 12)
    return {
        "tokens": noise(part_splits[0], (H2, W2, C2), 1.0, 6.0, ((0, 4), (1, 4))),
        "cotangent": noise(part_splits[1], (H2 // 2, W2 // 2, C3), 1.0, 6.0, ((0, 4), (1, 4))),
        "shift_offsets": plant(jax.random.randint(splits[2], (4,), 1, WIN), jax.random.fold_in(splits[2], 1), 1, WIN - 1).astype(jnp.int32),
        "norm2_gain": jnp.clip(1.0 + 0.18 * jax.random.normal(splits[3], (C2,), jnp.float32), 0.1, 1.9),
        "qkv2": noise(splits[4], (C2, 3 * C2), C2 ** -0.5, 0.375),
        "proj2": noise(splits[5], (C2, C2), C2 ** -0.5, 0.375),
        "merge_gain": jnp.clip(1.0 + 0.18 * jax.random.normal(splits[6], (4 * C2,), jnp.float32), 0.1, 1.9),
        "merge_weight": noise(splits[7], (4 * C2, C3), (4 * C2) ** -0.5, 0.1875),
        "norm3_gain": jnp.clip(1.0 + 0.18 * jax.random.normal(splits[8], (C3,), jnp.float32), 0.1, 1.9),
        "qkv3": noise(splits[9], (C3, 3 * C3), C3 ** -0.5, 0.25),
        "proj3": noise(splits[10], (C3, C3), C3 ** -0.5, 0.25),
    }


EPSILON = 1e-05
MASKED = -100.0

def normalize(inputs, gain):
    widened = inputs.astype(jnp.float32)
    centred = widened - lax.optimization_barrier(jnp.mean(widened, axis=-1, keepdims=True))
    spread = lax.optimization_barrier(jnp.mean(centred * centred, axis=-1, keepdims=True))
    return (centred * lax.rsqrt(spread + EPSILON) * gain).astype(jnp.bfloat16)

def attend(packed, heads, region):
    count, window_area, triple = packed.shape
    width = triple // 3
    head_size = width // heads
    queries = packed[:, :, :width].astype(jnp.float32).reshape(count, window_area, heads, head_size)
    key_part = packed[:, :, width:2 * width].astype(jnp.float32).reshape(count, window_area, heads, head_size)
    values = packed[:, :, 2 * width:].astype(jnp.float32).reshape(count, window_area, heads, head_size)
    scores = jnp.einsum('nphd,nqhd->nhpq', queries, key_part) * head_size ** (-0.5)
    scores = scores + region[:, None, :, :]
    raised = jnp.exp(scores)
    weights = (raised / lax.optimization_barrier(jnp.sum(raised, axis=-1, keepdims=True))).astype(jnp.bfloat16)
    mixed = jnp.einsum('nhpq,nqhd->nphd', weights.astype(jnp.float32), values)
    return mixed.reshape(count, window_area, width).astype(jnp.bfloat16)

def to_windows(values, window):
    height, breadth, width = values.shape
    shaped = values.reshape(height // window, window, breadth // window, window, width)
    return shaped.transpose(0, 2, 1, 3, 4).reshape(-1, window * window, width)

def from_windows(windows, height, breadth, window):
    width = windows.shape[-1]
    shaped = windows.reshape(height // window, breadth // window, window, window, width)
    return shaped.transpose(0, 2, 1, 3, 4).reshape(height, breadth, width)

def pair_join(values):
    height, breadth, width = values.shape
    shaped = values.reshape(height // 2, 2, breadth // 2, 2, width)
    return shaped.transpose(0, 2, 3, 1, 4).reshape(height // 2, breadth // 2, 4 * width)

def cyclic(values, start, axis):
    doubled = jnp.concatenate([values, values], axis=axis)
    return lax.dynamic_slice_in_dim(doubled, start.astype(jnp.int32), values.shape[axis], axis)

def region_bias(row_coords, col_coords, height, breadth, shift_rows, shift_cols):
    row_label = jnp.where(row_coords < height - WIN, 0, jnp.where(row_coords < height - shift_rows, 1, 2))
    col_label = jnp.where(col_coords < breadth - WIN, 0, jnp.where(col_coords < breadth - shift_cols, 1, 2))
    labels = (row_label[:, None] * 3 + col_label[None, :]).astype(jnp.int32)
    windowed = to_windows(labels[:, :, None], WIN)[:, :, 0]
    return jnp.where(windowed[:, :, None] == windowed[:, None, :], 0.0, MASKED).astype(jnp.float32)

def shifted_block(inputs, normed, shift_rows, shift_cols, qkv, proj, heads):
    height, breadth, width = inputs.shape
    rolled = to_windows(cyclic(cyclic(normed, shift_rows, 0), shift_cols, 1), WIN)
    bias = region_bias(jnp.arange(height, dtype=jnp.int32), jnp.arange(breadth, dtype=jnp.int32), height, breadth, shift_rows, shift_cols)
    packed = jnp.dot(rolled.reshape(-1, width), qkv, preferred_element_type=jnp.float32)
    packed = packed.astype(jnp.bfloat16).reshape(rolled.shape[0], WIN * WIN, 3 * width)
    mixed = attend(packed, heads, bias)
    projected = jnp.dot(mixed.reshape(-1, width), proj, preferred_element_type=jnp.float32).astype(jnp.bfloat16)
    grid = from_windows(projected.reshape(-1, WIN * WIN, width), height, breadth, WIN)
    restored = cyclic(cyclic(grid, height - shift_rows, 0), breadth - shift_cols, 1)
    return (inputs.astype(jnp.float32) + restored.astype(jnp.float32)).astype(jnp.bfloat16)

def forward(tokens, norm2_gain, qkv2, proj2, merge_gain, merge_weight, norm3_gain, qkv3, proj3, shift_offsets):
    height, breadth, narrow = tokens.shape
    wide_width = qkv3.shape[0]
    normed = normalize(tokens, norm2_gain)
    section_two = shifted_block(tokens, normed, shift_offsets[0], shift_offsets[1], qkv2, proj2, HEADS2)
    merged_norm = normalize(pair_join(section_two), merge_gain)
    merged = jnp.dot(merged_norm.reshape(-1, 4 * narrow), merge_weight, preferred_element_type=jnp.float32)
    merged = merged.astype(jnp.bfloat16).reshape(height // 2, breadth // 2, wide_width)
    normed_three = normalize(merged, norm3_gain)
    return shifted_block(merged, normed_three, shift_offsets[2], shift_offsets[3], qkv3, proj3, HEADS3)

def reference(tokens, cotangent, shift_offsets, norm2_gain, qkv2, proj2, merge_gain, merge_weight, norm3_gain, qkv3, proj3):

    def run(tok, gain_two, weight_qkv2, weight_proj2, gain_merge, weight_merge, gain_three, weight_qkv3, weight_proj3):
        return forward(tok, gain_two, weight_qkv2, weight_proj2, gain_merge, weight_merge, gain_three, weight_qkv3, weight_proj3, shift_offsets)
    outcome, pullback = jax.vjp(run, tokens, norm2_gain, qkv2, proj2, merge_gain, merge_weight, norm3_gain, qkv3, proj3)
    grads = pullback(cotangent)
    gains = jnp.concatenate([grads[1], grads[4], grads[6]])
    return (outcome, grads[0], gains, grads[2].reshape(-1), grads[3].reshape(-1), grads[5].reshape(-1), grads[7].reshape(-1), grads[8].reshape(-1))
```

```python
import functools

import jax
import jax.numpy as jnp
import numpy as np
from jax import lax
from jax.experimental import pallas as pl
from jax.experimental.pallas import tpu as pltpu
from jax.sharding import PartitionSpec as P

HEAD = 32
WIN = 7
MARGIN = WIN - 1
NEAR = 4
SLOT = 64
LANES = 128
EPSILON = 1e-05
MASKED = -100.0
F32 = jnp.float32
BF16 = jnp.bfloat16


def pitch_of(count):
    return -(-count // 16) * 16


def window_tokens(rows, cols):
    h, w, ok = [], [], []
    for wr in range(rows // WIN):
        for wc in range(cols // WIN):
            for t in range(SLOT):
                good = t < WIN * WIN
                h.append(wr * WIN + t // WIN if good else 0)
                w.append(wc * WIN + t % WIN if good else 0)
                ok.append(good)
    return np.array(h, np.int32), np.array(w, np.int32), np.array(ok)


def grid_tokens(rows, cols, pitch):
    h = np.repeat(np.arange(rows, dtype=np.int32), pitch)
    w = np.tile(np.arange(pitch, dtype=np.int32), rows)
    ok = w < cols
    return h, np.where(ok, w, 0).astype(np.int32), ok


def quad_tokens(rows, cols):
    a, b, ok = grid_tokens(rows // 2, cols // 2, pitch_of(cols // 2))
    h = np.concatenate([2 * a + (k & 1) for k in range(4)])
    w = np.concatenate([2 * b + (k >> 1) for k in range(4)])
    return h, w, np.tile(ok, 4)


def by_window(x):
    return (x * 9363) >> 16


def win_index(h, w, cols):
    hq, wq = by_window(h), by_window(w)
    return (hq * (cols // WIN) + wq) * SLOT + (h - hq * WIN) * WIN + w - wq * WIN


def quad_index(h, w, rows, cols):
    pitch = pitch_of(cols // 2)
    return ((h & 1) + 2 * (w & 1)) * ((rows // 2) * pitch) + (h >> 1) * pitch + (w >> 1)


def coded(tokens):
    h, w, ok = tokens
    return np.where(ok, h * 4096 + w, -1).astype(np.int32).reshape(-1, 1)


def decoded(code):
    return code >> 12, code & 4095, code >= 0


def padded(count):
    return -(-count // 16) * 16


class Shift:
    def __init__(self, rows, cols, margin, behind, pitch=None):
        self.rows, self.cols, self.margin, self.behind = rows, cols, margin, behind
        self.pitch = pitch or cols
        self.row = padded(margin * self.pitch)
        self.col = padded(rows * margin)
        self.first = (rows - margin) * margin // 16 * 16 if behind else 0
        self.corner = (self.col if behind else padded(margin * margin)) - self.first
        self.by = 1 if behind else -1
        self.extra = self.row + self.col + self.corner

    def sizes(self):
        return self.row, self.col, self.corner

    def index(self, code, by_rows, by_cols, inner, base):
        h, w, ok = decoded(code)
        m, rows, cols = self.margin, self.rows, self.cols
        if self.behind:
            h2, w2 = h - by_rows, w - by_cols
            local = inner(jnp.maximum(h2, 0), jnp.maximum(w2, 0))
            out_row, out_col = h2 < 0, w2 < 0
            r, c = h2 + m, w2 + m
            corner = (h2 + rows) * m - self.first + c
        else:
            h2, w2 = h + by_rows, w + by_cols
            local = inner(jnp.minimum(h2, rows - 1), jnp.minimum(w2, cols - 1))
            out_row, out_col = h2 >= rows, w2 >= cols
            r, c = h2 - rows, w2 - cols
            corner = r * m + c
        row = base + r * self.pitch + w2
        side = base + self.row + h2 * m + c
        corner = base + self.row + self.col + corner
        got = jnp.where(
            out_row, jnp.where(out_col, corner, row), jnp.where(out_col, side, local)
        )
        return jnp.where(ok, got, -1)

    def pieces(self, inner):
        m = self.margin
        top = self.rows - m if self.behind else 0
        left = self.cols - m if self.behind else 0
        parts = []
        for count, wide, pitch, h0, w0, size in (
            (m, self.cols, self.pitch, top, 0, self.row),
            (self.rows, m, m, 0, left, self.col),
        ):
            h, w, ok = grid_tokens(count, wide, pitch)
            got = np.where(ok, inner(h + h0, w + w0), -1)
            parts.append(np.pad(got, (0, size - len(got)), constant_values=-1))
        return np.concatenate(parts).astype(np.int32).reshape(-1, 1)


def window_labels(code, rows, cols, axis_row, axis_col, shift_rows, shift_cols):
    h, w, ok = decoded(code)
    height = rows * lax.axis_size("rows")
    breadth = cols * lax.axis_size("cols")
    gh = axis_row * rows + h
    gw = axis_col * cols + w
    lh = jnp.where(gh < height - WIN, 0, jnp.where(gh < height - shift_rows, 1, 2))
    lw = jnp.where(gw < breadth - WIN, 0, jnp.where(gw < breadth - shift_cols, 1, 2))
    return jnp.where(ok, lh * 3 + lw, -1)


def dot(a, b):
    return jnp.dot(a, b, preferred_element_type=F32)


def dot_nt(a, b):
    return lax.dot_general(a, b, (((1,), (1,)), ((), ())), preferred_element_type=F32)


def dot_tn(a, b):
    return lax.dot_general(a, b, (((0,), (0,)), ((), ())), preferred_element_type=F32)


def one_hot(idx, count):
    lane = lax.broadcasted_iota(jnp.int32, (idx.shape[0], count), 1)
    return jnp.where(idx == lane, 1.0, 0.0).astype(BF16)


def picked(hot, source):
    return dot(hot, source).astype(BF16)


def select(idx, source):
    return picked(one_hot(idx, source.shape[0]), source)


def norm_parts(x):
    centred = x - jnp.mean(x, axis=-1, keepdims=True)
    inverse = lax.rsqrt(jnp.mean(centred * centred, axis=-1, keepdims=True) + EPSILON)
    return centred * inverse, inverse


def norm_back(hat, inverse, gain, dy):
    grad_gain = jnp.sum(dy * hat, axis=0, keepdims=True)
    t = dy * gain
    dx = inverse * (
        t
        - jnp.mean(t, axis=-1, keepdims=True)
        - hat * jnp.mean(t * hat, axis=-1, keepdims=True)
    )
    return dx.astype(BF16), grad_gain


PACK = LANES // HEAD


def head_masks():
    lane = lax.broadcasted_iota(jnp.int32, (1, LANES), 1) // HEAD
    return [jnp.where(lane == h, 1.0, 0.0).astype(BF16) for h in range(PACK)]


def stack_heads(x, masks):
    return jnp.concatenate([x * m for m in masks], axis=0)


def pick_heads(o):
    lane = lax.broadcasted_iota(jnp.int32, (SLOT, LANES), 1) // HEAD
    out = o[:SLOT]
    for h in range(1, PACK):
        out = jnp.where(lane == h, o[h * SLOT : (h + 1) * SLOT], out)
    return out


def window_bias(lc_ref, lr_ref, w):
    lc = lc_ref[w * SLOT : (w + 1) * SLOT, :]
    lr = lr_ref[w : w + 1, :]
    bias = jnp.where((lc == lr) | (lc < 0), 0.0, MASKED)
    bias = jnp.where(lr < 0, -1e30, bias)
    return jnp.concatenate([bias] * PACK, axis=0)


def soft(qs, k, bias):
    raised = jnp.exp(dot_nt(qs, k) * HEAD ** (-0.5) + bias)
    return raised * (1.0 / jnp.sum(raised, axis=-1, keepdims=True))


def unit_back(qs, k, v, weights, wb, dm, masks):
    dms = stack_heads(dm, masks)
    dw = dot_nt(dms, v).astype(BF16).astype(F32)
    ds = weights * (dw - jnp.sum(dw * weights, axis=-1, keepdims=True))
    ds = (ds * HEAD ** (-0.5)).astype(BF16)
    dq = pick_heads(dot(ds, k))
    dk = dot_tn(ds, qs)
    dv = dot_tn(wb, dms)
    return dq.astype(BF16), dk.astype(BF16), dv.astype(BF16)


def fill_tile(scratch, tile, pitch):
    count, wide, _ = tile.shape
    for r in range(count):
        scratch[r * pitch : r * pitch + wide, :] = tile[r]


LATE = ("qkv2", "proj2", "weight", "proj3", "qkv3", )


class Load:
    def __init__(self, copy):
        self.copy, self.flying = copy, True
        copy.start()

    def wait(self):
        if self.flying:
            self.copy.wait()
        self.flying = False


class Bag:
    pass


MESH = pl.DeviceIdType.MESH


class Links:
    def __init__(self, send, recv):
        self.send, self.recv, self.used = send, recv, 0
        self.group = lax.axis_index("groups")
        self.row, self.col = lax.axis_index("rows"), lax.axis_index("cols")
        self.nr, self.nc = lax.axis_size("rows"), lax.axis_size("cols")
        self.core, self.chip = lax.rem(self.col, 2), self.col // 2
        self.chips = self.nc // 2

    def device(self, dr, dc):
        row = lax.rem(self.row + dr + self.nr, self.nr)
        col = lax.rem(self.col + dc + self.nc, self.nc)
        return (self.group, row, col)

    def partner(self):
        return (self.group, self.row, self.chip * 2 + 1 - self.core)

    def greet(self):
        offsets = {(d, 0) for d in range(1, self.nr)} | {(0, d) for d in range(1, self.nc)}
        offsets |= {(1, 1), (self.nr - 1, self.nc - 1)}
        self.greeted = len(offsets)
        sem = pltpu.get_barrier_semaphore()
        for dr, dc in sorted(offsets):
            pl.semaphore_signal(sem, inc=1, device_id=self.device(dr, dc), device_id_type=MESH)

    def barrier(self):
        pl.semaphore_wait(pltpu.get_barrier_semaphore(), self.greeted)

    def start(self, source, target, device):
        copy = pltpu.make_async_remote_copy(
            src_ref=source,
            dst_ref=target,
            send_sem=self.send.at[self.used],
            recv_sem=self.recv.at[self.used],
            device_id=device,
            device_id_type=MESH,
        )
        self.used += 1
        copy.start()
        return copy

    def exchange(self, shift, row, col, halo):
        by = shift.by
        corner = col.at[shift.first : shift.first + shift.corner]
        return [
            self.start(row, halo[0], self.device(by, 0)),
            self.start(corner, halo[2], self.device(by, by)),
            self.start(col, halo[1], self.device(0, by)),
        ]


def wait_all(copies):
    for copy in copies:
        copy.wait()


class Reduction:
    def __init__(self, links, kind, parts, bufs):
        self.links, self.kind, self.parts = links, kind, parts
        self.got1, self.half, self.got2, self.part, self.got3 = bufs
        self.arriving, self.sent, self.copies, self.step = {}, 1, [], 1


    def start_first(self, d):
        k = self.links
        x = lax.rem(k.chip + d, k.chips)
        return k.start(self.parts.at[1 - k.core, x], self.got1.at[x], k.partner())

    def first_away(self):
        self.away = [self.start_first(d) for d in range(1, self.links.chips)]

    def first_own(self):
        self.own = self.start_first(0)

    def both_cores(self, x, r):
        return self.parts[self.links.core, x, r].astype(F32) + self.got1[x, r].astype(F32)

    def second(self, steps=99):
        k = self.links
        if not self.arriving:
            wait_all(self.away)
        for e in range(self.sent, min(self.sent + steps, k.nr + 1)):
            r = lax.rem(k.row + e, k.nr)
            for d in range(1, k.chips):
                x = lax.rem(k.chip + d, k.chips)
                self.half[x, r] = self.both_cores(x, r).astype(self.kind)
                self.arriving[e, d] = k.start(
                    self.half.at[x, r], self.got2.at[d - 1, r], k.device(0, 2 * d)
                )
        self.sent += steps

    def third(self, steps=None):
        k = self.links
        if self.step == 1:
            self.own.wait()
        stop = k.nr + 1 if steps is None else min(self.step + steps, k.nr + 1)
        for e in range(self.step, stop):
            r = lax.rem(k.row + e, k.nr)
            total = self.both_cores(k.chip, r)
            for d in range(1, k.chips):
                self.arriving[e, d].wait()
                total = total + self.got2[d - 1, r].astype(F32)
            self.part[r] = total.astype(self.kind)
            if e < k.nr:
                self.copies.append(k.start(self.part.at[r], self.got3.at[e - 1], k.device(e, 0)))
        self.step = stop

    def finish(self):
        k = self.links
        wait_all(self.copies)
        total = self.part[k.row].astype(F32)
        for d in range(1, k.nr):
            total = total + self.got3[d - 1].astype(F32)
        return total


class GainSum:
    def __init__(self, links, bufs):
        self.links = links
        self.own, self.got1, self.half, self.got2, self.part, self.got3 = bufs

    def first(self):
        self.copies = [self.links.start(self.own, self.got1, self.links.partner())]

    def second(self):
        k = self.links
        wait_all(self.copies)
        self.half[...] = self.own[...] + self.got1[...]
        self.copies = [
            k.start(self.half, self.got2.at[d - 1], k.device(0, 2 * d)) for d in range(1, k.chips)
        ]

    def third(self):
        k = self.links
        wait_all(self.copies)
        total = self.half[...]
        for d in range(1, k.chips):
            total = total + self.got2[d - 1]
        self.part[...] = total
        self.copies = [k.start(self.part, self.got3.at[d - 1], k.device(d, 0)) for d in range(1, k.nr)]

    def finish(self):
        wait_all(self.copies)
        total = self.part[...]
        for d in range(1, self.links.nr):
            total = total + self.got3[d - 1]
        return total


def store_parts(parts, value, offset):
    _, chips, nr, depth, _ = parts.shape
    width = value.shape[1]
    for r in range(nr):
        for x in range(chips):
            for core in range(2):
                i = (r * chips + x) * 2 + core
                piece = value[i * depth : (i + 1) * depth]
                parts[core, x, r, :, offset : offset + width] = piece.astype(BF16)


def fill_side(scratch, tile, margin):
    scratch[...] = jnp.zeros_like(scratch)
    for r in range(tile.shape[0]):
        scratch[r * margin : (r + 1) * margin, :] = tile[r, :margin, :]


def put_pieces(idx, source, row_ref, col_ref):
    got = select(idx[...], source)
    row_ref[...] = got[: row_ref.shape[0]]
    col_ref[...] = got[row_ref.shape[0] :]


def lanes_of(width, g):
    return [slice(t * width + g * LANES, t * width + (g + 1) * LANES) for t in range(3)]


def shifts_of(rows, cols, rows3, cols3):
    pitch3 = pitch_of(cols3)
    return (
        Shift(rows, cols, MARGIN, False),
        Shift(rows3, cols3, MARGIN, False, pitch3),
        Shift(rows, cols, NEAR, True),
        Shift(rows3, cols3, MARGIN, False, pitch3),
        Shift(rows3, cols3, MARGIN, True),
        Shift(rows, cols, NEAR, False),
        Shift(rows, cols, MARGIN, True),
        Shift(rows3, cols3, MARGIN, True),
    )


class Pick:
    def __init__(self, idx, local, halo):
        base, extra = local.shape[0], sum(h.shape[0] for h in halo)
        self.part = dot(one_hot(idx, base), local)
        self.hot = one_hot(idx - base, extra)
        self.halo = halo

    def finish(self, flying, at=slice(None)):
        wait_all(flying)
        rest = jnp.concatenate([h[...] for h in self.halo], axis=0)
        return (self.part[at] + dot(self.hot[at], rest)).astype(BF16)


def early_windows(rows, cols, margin):
    if 2 * WIN + margin > rows + WIN:
        return 0
    return (cols - margin) // WIN


def whole_kernel(in_names, out_names, scratch_names, *refs):
    b = Bag()
    for name, ref in zip(in_names + out_names + scratch_names, refs, strict=True):
        setattr(b, name, ref)
    links = Links(b.send, b.recv)
    links.greet()
    loads = {}
    for n, name in enumerate(LATE):
        kept = getattr(b, "v_" + name)
        loads[name] = Load(pltpu.make_async_copy(getattr(b, name), kept, b.loaded.at[n]))
        setattr(b, name, kept)
    rows, cols, narrow = b.tok.shape
    rows3, cols3, wide = b.cot.shape
    pitch, pitch3 = pitch_of(cols), pitch_of(cols3)
    red3 = Reduction(links, BF16, b.g3, [getattr(b, f"g3_{i}") for i in range(5)])
    redm = Reduction(links, BF16, b.gm, [getattr(b, f"gm_{i}") for i in range(5)])
    red2 = Reduction(links, BF16, b.g2, [getattr(b, f"g2_{i}") for i in range(5)])
    redg = GainSum(links, [getattr(b, f"gg_{i}") for i in range(6)])
    ways = shifts_of(rows, cols, rows3, cols3)
    halos = [[getattr(b, f"h{n}_{i}") for i in range(3)] for n in range(len(ways))]
    row_of = [getattr(b, f"row{n}") if hasattr(b, f"row{n}") else None for n in range(len(ways))]
    col_of = [getattr(b, f"col{n}") for n in range(len(ways))]
    masks = head_masks()
    s0, s1, s2, s3 = (b.shifts[i] for i in range(4))
    e0 = jnp.minimum(s0 - (s0 & 1), 2 * s2)
    e1 = jnp.minimum(s1 - (s1 & 1), 2 * s3)
    t0, t1 = s0 - e0, s1 - e1
    d0, d1 = s2 - (e0 >> 1), s3 - (e1 >> 1)
    quads, n2, n3 = b.quad.shape[0], b.win2.shape[0], b.win3.shape[0]
    base, base3 = b.toks.shape[0], rows3 * pitch3
    as_toks = lambda h, w: h * cols + w
    as_grid3 = lambda h, w: h * pitch3 + w
    as_quad = lambda h, w: quad_index(h, w, rows, cols)
    as_win = lambda h, w: win_index(h, w, cols)
    as_win3 = lambda h, w: win_index(h, w, cols3)

    for n, way in enumerate(ways):
        way.number = n

    def exchange(n, row=None):
        row = row_of[n] if row is None else row
        return links.exchange(ways[n], row, col_of[n], halos[n])

    if base > rows * cols:
        b.toks[rows * cols :, :] = jnp.zeros((base - rows * cols, narrow), BF16)
    fill_tile(b.toks, b.tok, cols)
    fill_side(b.col0, b.tok, MARGIN)
    b.cots[...] = jnp.zeros_like(b.cots)
    fill_tile(b.cots, b.cot, pitch3)
    fill_side(b.col1, b.cot, MARGIN)
    links.barrier()
    flying = exchange(0, b.toks.at[0 : ways[0].row])
    flying_c = exchange(1, b.cots.at[0 : ways[1].row])

    pick = Pick(ways[0].index(b.win2[...], s0, s1, as_toks, base), b.toks[...], halos[0])
    place2 = (rows, cols, links.row, links.col, s0, s1)
    place3 = (rows3, cols3, links.row, links.col, s2, s3)
    b.lc2[...] = window_labels(b.win2[...], *place2)
    b.lr2[...] = window_labels(b.rwin2[...], *place2)
    b.lc3[...] = window_labels(b.win3[...], *place3)
    b.lr3[...] = window_labels(b.rwin3[...], *place3)
    early = early_windows(rows, cols, MARGIN)
    for half in (range(early), range(early, n2 // SLOT)):
        part = slice(half.start * SLOT, half.stop * SLOT)
        tok2 = pick.finish(flying, part) if half.start else pick.part[part].astype(BF16)
        b.tok2[part] = tok2
        hat, _ = norm_parts(tok2.astype(F32))
        b.rolled[part] = (hat * b.gain2[...]).astype(BF16)
        if half.start == 0:
            loads["qkv2"].wait()
        b.packed[part] = dot(b.rolled[part], b.qkv2[...]).astype(BF16)
        for w in half:
            bias = window_bias(b.lc2, b.lr2, w)
            at = slice(w * SLOT, (w + 1) * SLOT)
            for g in range(narrow // LANES):
                lanes = lanes_of(narrow, g)
                qs = stack_heads(b.packed[at, lanes[0]], masks)
                weights = soft(qs, b.packed[at, lanes[1]], bias)
                b.kept[w * (narrow // LANES) + g] = weights
                wb = weights.astype(BF16)
                b.mixed[at, lanes[0]] = pick_heads(dot(wb, b.packed[at, lanes[2]])).astype(BF16)
    loads["proj2"].wait()
    win = dot(b.mixed[...], b.proj2[...]).astype(BF16)
    section = (b.tok2[...].astype(F32) + win.astype(F32)).astype(BF16)
    put_pieces(b.idx2, section, b.row2, b.col2)
    flying = exchange(2)

    pick = Pick(ways[2].index(b.quad[...], t0, t1, as_win, n2), section, halos[2])
    pick_c = Pick(ways[1].index(b.win3[...], s2, s3, as_grid3, base3), b.cots[...], halos[1])
    section = pick.finish(flying)
    t3 = rows3 * pitch3
    joined = jnp.concatenate([section[k * t3 : (k + 1) * t3] for k in range(4)], axis=1)
    b.joined[...] = joined
    hat, _ = norm_parts(joined.astype(F32))
    b.mnorm[...] = (hat * b.gainm[...]).astype(BF16)
    loads["weight"].wait()
    merged = dot(b.mnorm[...], b.weight[...]).astype(BF16)
    b.merged[...] = merged
    b.col3[...] = jnp.zeros_like(b.col3)
    for r in range(rows3):
        b.col3[r * MARGIN : (r + 1) * MARGIN, :] = merged[r * pitch3 : r * pitch3 + MARGIN]
    flying = exchange(3, b.merged.at[0 : ways[3].row])

    pick = Pick(ways[3].index(b.win3[...], d0, d1, as_grid3, base3), merged, halos[3])
    b.dproj3[...] = pick_c.finish(flying_c)
    loads["proj3"].wait()
    dmixed = dot_nt(b.dproj3[...], b.proj3[...]).astype(BF16)
    merged3 = pick.finish(flying)
    b.merged3[...] = merged3
    hat, _ = norm_parts(merged3.astype(F32))
    rolled3 = (hat * b.gain3[...]).astype(BF16)
    b.rolled3[...] = rolled3
    loads["qkv3"].wait()
    b.packed3[...] = dot(rolled3, b.qkv3[...]).astype(BF16)
    for w in range(b.lr3.shape[0]):
        bias = window_bias(b.lc3, b.lr3, w)
        at = slice(w * SLOT, (w + 1) * SLOT)
        for g in range(wide // LANES):
            lanes = lanes_of(wide, g)
            qs = stack_heads(b.packed3[at, lanes[0]], masks)
            k, v = b.packed3[at, lanes[1]], b.packed3[at, lanes[2]]
            weights = soft(qs, k, bias)
            wb = weights.astype(BF16)
            b.mixed3[at, lanes[0]] = pick_heads(dot(wb, v)).astype(BF16)
            back = unit_back(qs, k, v, weights, wb, dmixed[at, lanes[0]], masks)
            for t in range(3):
                b.dpacked3[at, lanes[t]] = back[t]
    drolled3 = dot_nt(b.dpacked3[...], b.qkv3[...]).astype(BF16)
    hat, inv = norm_parts(b.merged3[...].astype(F32))
    dmerged3, grad3 = norm_back(hat, inv, b.gain3[...], drolled3.astype(F32))
    dmerged3 = b.dproj3[...] + dmerged3
    put_pieces(b.idx4, dmerged3, b.row4, b.col4)
    flying = exchange(4)
    store_parts(b.g3, dot_tn(b.rolled3[...], b.dpacked3[...]), 0)
    store_parts(b.g3, dot_tn(b.mixed3[...], b.dproj3[...]), 3 * wide)
    red3.first_away()
    red3.first_own()
    proj = dot(b.mixed3[...], b.proj3[...]).astype(BF16)
    out3 = (b.merged3[...].astype(F32) + proj.astype(F32)).astype(BF16)
    put_pieces(b.idx7, out3, b.row7, b.col7)
    flying_o = exchange(7)
    pick_o = Pick(ways[7].index(b.grid3[...], s2, s3, as_win3, n3), out3, halos[7])
    pick = Pick(ways[4].index(b.grid3[...], d0, d1, as_win3, n3), dmerged3, halos[4])
    red3.second(1)
    hat, inv = norm_parts(b.joined[...].astype(F32))
    dmerged = pick.finish(flying)
    djn = dot_nt(dmerged, b.weight[...]).astype(BF16).astype(F32)
    djoined, gradm = norm_back(hat, inv, b.gainm[...], djn)
    b.gg_0[:, narrow : 5 * narrow] = gradm
    b.gg_0[:, 5 * narrow :] = grad3
    b.dsec[...] = jnp.concatenate(
        [djoined[:, k * narrow : (k + 1) * narrow] for k in range(4)], axis=0
    )
    put_pieces(b.idx5, b.dsec[...], b.row5, b.col5)
    flying = exchange(5)
    store_parts(b.gm, dot_tn(b.mnorm[...], dmerged), 0)
    redm.first_away()
    redm.first_own()
    red3.second()
    pick = Pick(ways[5].index(b.win2[...], t0, t1, as_quad, quads), b.dsec[...], halos[5])
    early = early_windows(rows, cols, NEAR)
    halves = [range(early), range(early, n2 // SLOT)]
    for half in halves:
        part = slice(half.start * SLOT, half.stop * SLOT)
        if half.start == 0:
            b.dsec2[part] = pick.part[part].astype(BF16)
        else:
            b.dsec2[part] = pick.finish(flying, part)
        dmixed = dot_nt(b.dsec2[part], b.proj2[...]).astype(BF16)
        for w in half:
            at = slice(w * SLOT, (w + 1) * SLOT)
            here = slice(at.start - part.start, at.stop - part.start)
            for g in range(narrow // LANES):
                lanes = lanes_of(narrow, g)
                qs = stack_heads(b.packed[at, lanes[0]], masks)
                k, v = b.packed[at, lanes[1]], b.packed[at, lanes[2]]
                weights = b.kept[w * (narrow // LANES) + g]
                back = unit_back(
                    qs, k, v, weights, weights.astype(BF16), dmixed[here, lanes[0]], masks
                )
                for t in range(3):
                    b.dpacked[at, lanes[t]] = back[t]
            if w == 0:
                redm.second()
            if w in (2, 3, 4):
                red3.third(1)
    drolled = dot_nt(b.dpacked[...], b.qkv2[...]).astype(BF16)
    hat, inv = norm_parts(b.tok2[...].astype(F32))
    dtok2, grad2 = norm_back(hat, inv, b.gain2[...], drolled.astype(F32))
    dtok2 = b.dsec2[...] + dtok2
    put_pieces(b.idx6, dtok2, b.row6, b.col6)
    flying = exchange(6)
    b.gg_0[:, :narrow] = grad2
    redg.first()
    store_parts(b.g2, dot_tn(b.rolled[...], b.dpacked[...]), 0)
    store_parts(b.g2, dot_tn(b.mixed[...], b.dsec2[...]), 3 * narrow)
    redg.second()
    red2.first_away()
    red2.first_own()
    red3.third()
    total = pick_o.finish(flying_o)
    for r in range(rows3):
        b.out[r] = total[r * pitch3 : r * pitch3 + cols3]
    red2.second()
    pick = Pick(ways[6].index(b.nat[...], s0, s1, as_win, n2), dtok2, halos[6])
    total = pick.finish(flying)
    for r in range(rows):
        b.dtok[r] = total[r * pitch : r * pitch + cols]
    redg.third()
    redm.third()
    red2.third()
    b.sum3[...] = red3.finish().astype(BF16)
    b.summ[...] = redm.finish().astype(BF16)
    b.sum2[...] = red2.finish().astype(BF16)
    b.gains[...] = redg.finish()


def finish_kernel(out, dtok, gains, sum3, summ, sum2, o_out, o_dtok, o_gains, *rest):
    o_out[...] = out[...]
    o_dtok[...] = dtok[...]
    for j in range(o_gains.shape[0]):
        o_gains[j : j + 1, :] = gains[:, j * LANES : (j + 1) * LANES]
    flats, rooms = rest[: len(rest) // 2], rest[len(rest) // 2 :]
    wide, narrow = sum3.shape[1] // 4, sum2.shape[1] // 4
    views = (
        (sum2, 0, 3 * narrow), (sum2, 3 * narrow, narrow), (summ, 0, wide),
        (sum3, 0, 3 * wide), (sum3, 3 * wide, wide),
    )
    for (source, offset, width), flat, room in zip(views, flats, rooms, strict=True):
        steps = width // LANES
        for j in range(steps):
            piece = source[:, offset + j * LANES : offset + (j + 1) * LANES]
            room[pl.ds(j, source.shape[0], stride=steps), :] = piece.astype(F32)
        flat[...] = room[...].astype(BF16)


def on_device(
    tokens, cotangent, shifts, norm2_gain, qkv2, proj2, merge_gain, merge_weight, norm3_gain,
    qkv3, proj3,
):
    rows, cols, narrow = tokens.shape
    wide = qkv3.shape[0]
    rows3, cols3 = rows // 2, cols // 2
    pitch, pitch3 = pitch_of(cols), pitch_of(cols3)
    base, base3 = padded(rows * cols), rows3 * pitch3
    win2, win3 = window_tokens(rows, cols), window_tokens(rows3, cols3)
    n2, n3 = len(win2[0]), len(win3[0])
    quad = quad_tokens(rows, cols)
    nat = grid_tokens(rows, cols, pitch)
    grid3 = grid_tokens(rows3, cols3, pitch3)
    as_quad = lambda h, w: quad_index(h, w, rows, cols)
    as_win = lambda h, w: win_index(h, w, cols)
    as_win3 = lambda h, w: win_index(h, w, cols3)
    ways = shifts_of(rows, cols, rows3, cols3)
    gain2, gainm, gain3 = (g.reshape(1, -1) for g in (norm2_gain, merge_gain, norm3_gain))
    nr, nc = lax.axis_size("rows"), lax.axis_size("cols")
    chips = nc // 2
    quads, gains = len(quad[0]), 5 * narrow + wide
    inputs = dict(
        tok=tokens, cot=cotangent, shifts=shifts, win2=coded(win2), win3=coded(win3),
        rwin2=coded(win2).reshape(-1, SLOT), rwin3=coded(win3).reshape(-1, SLOT),
        quad=coded(quad), nat=coded(nat), grid3=coded(grid3),
        idx2=ways[2].pieces(as_win), idx4=ways[4].pieces(as_win3), idx5=ways[5].pieces(as_quad),
        idx6=ways[6].pieces(as_win), idx7=ways[7].pieces(as_win3),
        gain2=gain2, gainm=gainm, gain3=gain3, qkv2=qkv2, proj2=proj2,
        weight=merge_weight, qkv3=qkv3, proj3=proj3,
    )
    m3, mm, m2 = wide // (nr * nc), 4 * narrow // (nr * nc), narrow // (nr * nc)
    outs = dict(
        out=(cotangent.shape, BF16),
        dtok=(tokens.shape, BF16),
        gains=((1, gains), F32),
        sum3=((m3, 4 * wide), BF16),
        summ=((mm, wide), BF16),
        sum2=((m2, 4 * narrow), BF16),
    )
    scratch = dict(
        toks=((base, narrow), BF16), cots=((base3, wide), BF16),
        tok2=((n2, narrow), BF16),
        rolled=((n2, narrow), BF16), packed=((n2, 3 * narrow), BF16), mixed=((n2, narrow), BF16),
        joined=((base3, 4 * narrow), BF16), mnorm=((base3, 4 * narrow), BF16),
        merged=((base3, wide), BF16), merged3=((n3, wide), BF16), rolled3=((n3, wide), BF16),
        dproj3=((n3, wide), BF16),
        packed3=((n3, 3 * wide), BF16), mixed3=((n3, wide), BF16),
        dpacked3=((n3, 3 * wide), BF16), dsec=((quads, narrow), BF16),
        dsec2=((n2, narrow), BF16), dpacked=((n2, 3 * narrow), BF16),
    )
    kept = (n2 // SLOT * (narrow // LANES), PACK * SLOT, SLOT)
    ints = dict(lc2=(n2, 1), lr2=(n2 // SLOT, SLOT), lc3=(n3, 1), lr3=(n3 // SLOT, SLOT))
    scratch |= {name: (shape, jnp.int32) for name, shape in ints.items()}
    scratch["kept"] = (kept, F32)
    for name in LATE:
        scratch["v_" + name] = (inputs[name].shape, inputs[name].dtype)
    copies = len(ways) * 3
    for n, way in enumerate(ways):
        width = narrow if way.rows == rows else wide
        if n not in (0, 1, 3):
            scratch[f"row{n}"] = ((way.row, width), BF16)
        scratch[f"col{n}"] = ((way.col, width), BF16)
        for i, size in enumerate(way.sizes()):
            scratch[f"h{n}_{i}"] = ((size, width), BF16)
    for name, shape in (("g3", (m3, 4 * wide)), ("gm", (mm, wide)), ("g2", (m2, 4 * narrow))):
        scratch[name] = ((2, chips, nr) + shape, BF16)
        for i, lead in enumerate(
            ((chips, nr), (chips, nr), (max(chips - 1, 1), nr), (nr,), (max(nr - 1, 1),))
        ):
            scratch[f"{name}_{i}"] = (lead + shape, BF16)
        copies += chips + (chips - 1) * nr + nr - 1
    for i, lead in enumerate(((), (), (), (max(chips - 1, 1),), (), (max(nr - 1, 1),))):
        scratch[f"gg_{i}"] = (lead + (1, gains), F32)
    copies += chips + nr - 1
    spaces = [pltpu.VMEM(s, d) for s, d in scratch.values()]
    spaces += [pltpu.SemaphoreType.DMA((n,)) for n in (copies, copies, len(LATE))]
    results = pl.pallas_call(
        functools.partial(
            whole_kernel, list(inputs), list(outs), list(scratch) + ["send", "recv", "loaded"]
        ),
        out_shape=[jax.ShapeDtypeStruct(s, d) for s, d in outs.values()],
        in_specs=[
            pl.BlockSpec(
                memory_space=pltpu.SMEM if name == "shifts" else pl.ANY if name in LATE else pltpu.VMEM
            )
            for name in inputs
        ],
        out_specs=[pl.BlockSpec(memory_space=pltpu.VMEM)] * len(outs),
        scratch_shapes=spaces,
        compiler_params=pltpu.CompilerParams(
            collective_id=0, has_side_effects=True, vmem_limit_bytes=60 * 2**20
        ),
        name="block",
    )(*inputs.values())
    flats = [
        (m * width // LANES, LANES)
        for m, width in (
            (m2, 3 * narrow), (m2, narrow), (mm, wide), (m3, 3 * wide), (m3, wide)
        )
    ]
    final = pl.pallas_call(
        finish_kernel,
        out_shape=[
            jax.ShapeDtypeStruct(cotangent.shape, BF16),
            jax.ShapeDtypeStruct(tokens.shape, BF16),
            jax.ShapeDtypeStruct((gains // LANES, LANES), F32),
        ]
        + [jax.ShapeDtypeStruct(shape, BF16) for shape in flats],
        scratch_shapes=[pltpu.VMEM(shape, F32) for shape in flats],
        name="finish",
    )(*results)
    return tuple(final[:2]) + tuple(x.reshape(-1) for x in final[2:])


def solution(mesh):
    tile = P(("groups", "rows"), "cols", None)
    spread = P(("groups", "rows", "cols"))
    return jax.shard_map(
        on_device,
        mesh=mesh,
        in_specs=(tile, tile) + (P(),) * 9,
        out_specs=(tile, tile, P("groups")) + (spread,) * 5,
        check_vma=False,
    )
```

```python
import functools

import jax
import jax.numpy as jnp
import numpy as np
from jax import lax
from jax.experimental import pallas as pl
from jax.experimental.pallas import tpu as pltpu
from jax.sharding import PartitionSpec as P

HEAD = 32
WIN = 7
MARGIN = WIN - 1
NEAR = 4
SLOT = 64
LANES = 128
EPSILON = 1e-05
MASKED = -100.0
F32 = jnp.float32
BF16 = jnp.bfloat16


def pitch_of(count):
    return -(-count // 16) * 16


def window_tokens(rows, cols):
    h, w, ok = [], [], []
    for wr in range(rows // WIN):
        for wc in range(cols // WIN):
            for t in range(SLOT):
                good = t < WIN * WIN
                h.append(wr * WIN + t // WIN if good else 0)
                w.append(wc * WIN + t % WIN if good else 0)
                ok.append(good)
    return np.array(h, np.int32), np.array(w, np.int32), np.array(ok)


def grid_tokens(rows, cols, pitch):
    h = np.repeat(np.arange(rows, dtype=np.int32), pitch)
    w = np.tile(np.arange(pitch, dtype=np.int32), rows)
    ok = w < cols
    return h, np.where(ok, w, 0).astype(np.int32), ok


def quad_tokens(rows, cols):
    a, b, ok = grid_tokens(rows // 2, cols // 2, pitch_of(cols // 2))
    h = np.concatenate([2 * a + (k & 1) for k in range(4)])
    w = np.concatenate([2 * b + (k >> 1) for k in range(4)])
    return h, w, np.tile(ok, 4)


def by_window(x):
    return (x * 9363) >> 16


def win_index(h, w, cols):
    hq, wq = by_window(h), by_window(w)
    return (hq * (cols // WIN) + wq) * SLOT + (h - hq * WIN) * WIN + w - wq * WIN


def quad_index(h, w, rows, cols):
    pitch = pitch_of(cols // 2)
    return ((h & 1) + 2 * (w & 1)) * ((rows // 2) * pitch) + (h >> 1) * pitch + (w >> 1)


def spread(values):
    return np.repeat(values.astype(np.int32).reshape(-1, 1), LANES, axis=1)


def coded(tokens):
    h, w, ok = tokens
    return spread(np.where(ok, h * 4096 + w, -1))


def decoded(code):
    return code >> 12, code & 4095, code >= 0


def padded(count):
    return -(-count // 16) * 16


class Shift:
    def __init__(self, rows, cols, margin, behind, pitch=None):
        self.rows, self.cols, self.margin, self.behind = rows, cols, margin, behind
        self.pitch = pitch or cols
        self.row = padded(margin * self.pitch)
        self.col = padded(rows * margin)
        self.first = (rows - margin) * margin // 16 * 16 if behind else 0
        self.corner = (self.col if behind else padded(margin * margin)) - self.first
        self.by = 1 if behind else -1
        self.extra = self.row + self.col + self.corner

    def sizes(self):
        return self.row, self.col, self.corner

    def index(self, code, by_rows, by_cols, inner, base):
        h, w, ok = decoded(code)
        m, rows, cols = self.margin, self.rows, self.cols
        if self.behind:
            h2, w2 = h - by_rows, w - by_cols
            local = inner(jnp.maximum(h2, 0), jnp.maximum(w2, 0))
            out_row, out_col = h2 < 0, w2 < 0
            r, c = h2 + m, w2 + m
            corner = (h2 + rows) * m - self.first + c
        else:
            h2, w2 = h + by_rows, w + by_cols
            local = inner(jnp.minimum(h2, rows - 1), jnp.minimum(w2, cols - 1))
            out_row, out_col = h2 >= rows, w2 >= cols
            r, c = h2 - rows, w2 - cols
            corner = r * m + c
        row = base + r * self.pitch + w2
        side = base + self.row + h2 * m + c
        corner = base + self.row + self.col + corner
        got = jnp.where(
            out_row, jnp.where(out_col, corner, row), jnp.where(out_col, side, local)
        )
        return jnp.where(ok, got, -1)

    def pieces(self, inner):
        m = self.margin
        top = self.rows - m if self.behind else 0
        left = self.cols - m if self.behind else 0
        parts = []
        for count, wide, pitch, h0, w0, size in (
            (m, self.cols, self.pitch, top, 0, self.row),
            (self.rows, m, m, 0, left, self.col),
        ):
            h, w, ok = grid_tokens(count, wide, pitch)
            got = np.where(ok, inner(h + h0, w + w0), -1)
            parts.append(np.pad(got, (0, size - len(got)), constant_values=-1))
        return spread(np.concatenate(parts))


def window_labels(code, rows, cols, axis_row, axis_col, shift_rows, shift_cols):
    h, w, ok = decoded(code)
    height = rows * lax.axis_size("rows")
    breadth = cols * lax.axis_size("cols")
    gh = axis_row * rows + h
    gw = axis_col * cols + w
    lh = jnp.where(gh < height - WIN, 0, jnp.where(gh < height - shift_rows, 1, 2))
    lw = jnp.where(gw < breadth - WIN, 0, jnp.where(gw < breadth - shift_cols, 1, 2))
    return jnp.where(ok, lh * 3 + lw, -1)


def dot(a, b):
    return jnp.dot(a, b, preferred_element_type=F32)


def dot_nt(a, b):
    return lax.dot_general(a, b, (((1,), (1,)), ((), ())), preferred_element_type=F32)


def dot_tn(a, b):
    return lax.dot_general(a, b, (((0,), (0,)), ((), ())), preferred_element_type=F32)


def one_hot(idx, count):
    lane = lax.broadcasted_iota(jnp.int32, (1, LANES), 1)
    parts = []
    for start in range(0, count, LANES):
        wide = min(LANES, count - start)
        parts.append(jnp.where(idx[:, :wide] == lane[:, :wide] + start, 1.0, 0.0).astype(BF16))
    return jnp.concatenate(parts, axis=1)


def picked(hot, source):
    return dot(hot, source).astype(BF16)


def select(idx, source):
    return picked(one_hot(idx, source.shape[0]), source)


def norm_parts(x):
    centred = x - jnp.mean(x, axis=-1, keepdims=True)
    inverse = lax.rsqrt(jnp.mean(centred * centred, axis=-1, keepdims=True) + EPSILON)
    return centred * inverse, inverse


def norm_back(hat, inverse, gain, dy):
    grad_gain = jnp.sum(dy * hat, axis=0, keepdims=True)
    t = dy * gain
    dx = inverse * (
        t
        - jnp.mean(t, axis=-1, keepdims=True)
        - hat * jnp.mean(t * hat, axis=-1, keepdims=True)
    )
    return dx.astype(BF16), grad_gain


PACK = LANES // HEAD


def head_masks():
    lane = lax.broadcasted_iota(jnp.int32, (1, LANES), 1) // HEAD
    return [jnp.where(lane == h, 1.0, 0.0).astype(BF16) for h in range(PACK)]


def stack_heads(x, masks):
    return jnp.concatenate([x * m for m in masks], axis=0)


def pick_heads(o):
    lane = lax.broadcasted_iota(jnp.int32, (SLOT, LANES), 1) // HEAD
    out = o[:SLOT]
    for h in range(1, PACK):
        out = jnp.where(lane == h, o[h * SLOT : (h + 1) * SLOT], out)
    return out


def window_bias(lc_ref, lr_ref, w):
    lc = lc_ref[w * SLOT : (w + 1) * SLOT, :]
    lr = lr_ref[w : w + 1, :]
    bias = jnp.where((lc == lr) | (lc < 0), 0.0, MASKED)
    bias = jnp.where(lr < 0, -1e30, bias)
    return jnp.concatenate([bias] * PACK, axis=0)


def soft(qs, k, bias):
    raised = jnp.exp(dot_nt(qs, k) * HEAD ** (-0.5) + bias)
    return raised * (1.0 / jnp.sum(raised, axis=-1, keepdims=True))


def unit_back(qs, k, v, weights, wb, dm, masks):
    dms = stack_heads(dm, masks)
    dw = dot_nt(dms, v).astype(BF16).astype(F32)
    ds = weights * (dw - jnp.sum(dw * weights, axis=-1, keepdims=True))
    ds = (ds * HEAD ** (-0.5)).astype(BF16)
    dq = pick_heads(dot(ds, k))
    dk = dot_tn(ds, qs)
    dv = dot_tn(wb, dms)
    return dq.astype(BF16), dk.astype(BF16), dv.astype(BF16)


def fill_tile(scratch, tile, pitch):
    count, wide, _ = tile.shape
    for r in range(count):
        scratch[r * pitch : r * pitch + wide, :] = tile[r]


LATE = ("qkv2", "proj2", "weight", "proj3", "qkv3", )


class Load:
    def __init__(self, copy):
        self.copy, self.flying = copy, True
        copy.start()

    def wait(self):
        if self.flying:
            self.copy.wait()
        self.flying = False


class Bag:
    pass


MESH = pl.DeviceIdType.MESH


class Links:
    def __init__(self, send, recv):
        self.send, self.recv, self.used = send, recv, 0
        self.group = lax.axis_index("groups")
        self.row, self.col = lax.axis_index("rows"), lax.axis_index("cols")
        self.nr, self.nc = lax.axis_size("rows"), lax.axis_size("cols")
        self.core, self.chip = lax.rem(self.col, 2), self.col // 2
        self.chips = self.nc // 2

    def device(self, dr, dc):
        row = lax.rem(self.row + dr + self.nr, self.nr)
        col = lax.rem(self.col + dc + self.nc, self.nc)
        return (self.group, row, col)

    def partner(self):
        return (self.group, self.row, self.chip * 2 + 1 - self.core)

    def greet(self):
        offsets = {(d, 0) for d in range(1, self.nr)} | {(0, d) for d in range(1, self.nc)}
        offsets |= {(1, 1), (self.nr - 1, self.nc - 1)}
        self.greeted = len(offsets)
        sem = pltpu.get_barrier_semaphore()
        for dr, dc in sorted(offsets):
            pl.semaphore_signal(sem, inc=1, device_id=self.device(dr, dc), device_id_type=MESH)

    def barrier(self):
        pl.semaphore_wait(pltpu.get_barrier_semaphore(), self.greeted)

    def start(self, source, target, device):
        copy = pltpu.make_async_remote_copy(
            src_ref=source,
            dst_ref=target,
            send_sem=self.send.at[self.used],
            recv_sem=self.recv.at[self.used],
            device_id=device,
            device_id_type=MESH,
        )
        self.used += 1
        copy.start()
        return copy

    def exchange(self, shift, row, col, halo):
        by = shift.by
        corner = col.at[shift.first : shift.first + shift.corner]
        return [
            self.start(row, halo[0], self.device(by, 0)),
            self.start(corner, halo[2], self.device(by, by)),
            self.start(col, halo[1], self.device(0, by)),
        ]


def wait_all(copies):
    for copy in copies:
        copy.wait()


class Reduction:
    def __init__(self, links, kind, parts, bufs, whole=False):
        self.links, self.kind, self.parts, self.whole = links, kind, parts, whole
        self.got1, self.half, self.got2, self.part, self.got3 = bufs
        self.arriving, self.sent, self.copies, self.step = {}, 1, [], 1


    def start_first(self, d):
        k = self.links
        x = lax.rem(k.chip + d, k.chips)
        return k.start(self.parts.at[1 - k.core, x], self.got1.at[x], k.partner())

    def first_away(self):
        k = self.links
        if self.whole:
            self.own = k.start(self.parts.at[1 - k.core], self.got1, k.partner())
            self.away = [self.own]
        else:
            self.away = [self.start_first(d) for d in range(1, k.chips)]

    def first_own(self):
        if not self.whole:
            self.own = self.start_first(0)

    def both_cores(self, x, r):
        return self.parts[self.links.core, x, r].astype(F32) + self.got1[x, r].astype(F32)

    def second(self, steps=99):
        k = self.links
        if self.whole:
            wait_all(self.away)
            for d in range(1, k.chips):
                x = lax.rem(k.chip + d, k.chips)
                for r in range(k.nr):
                    self.half[x, r] = self.both_cores(x, r).astype(self.kind)
                self.arriving[1, d] = k.start(
                    self.half.at[x], self.got2.at[d - 1], k.device(0, 2 * d)
                )
            return
        if not self.arriving:
            wait_all(self.away)
        for e in range(self.sent, min(self.sent + steps, k.nr + 1)):
            r = lax.rem(k.row + e, k.nr)
            for d in range(1, k.chips):
                x = lax.rem(k.chip + d, k.chips)
                self.half[x, r] = self.both_cores(x, r).astype(self.kind)
                self.arriving[e, d] = k.start(
                    self.half.at[x, r], self.got2.at[d - 1, r], k.device(0, 2 * d)
                )
        self.sent += steps

    def third(self, steps=None):
        k = self.links
        if self.step == 1 and not self.whole:
            self.own.wait()
        stop = k.nr + 1 if steps is None else min(self.step + steps, k.nr + 1)
        for e in range(self.step, stop):
            r = lax.rem(k.row + e, k.nr)
            total = self.both_cores(k.chip, r)
            for d in range(1, k.chips):
                if (e, d) in self.arriving:
                    self.arriving[e, d].wait()
                total = total + self.got2[d - 1, r].astype(F32)
            self.part[r] = total.astype(self.kind)
            if e < k.nr:
                self.copies.append(k.start(self.part.at[r], self.got3.at[e - 1], k.device(e, 0)))
        self.step = stop

    def finish(self):
        k = self.links
        wait_all(self.copies)
        total = self.part[k.row].astype(F32)
        for d in range(1, k.nr):
            total = total + self.got3[d - 1].astype(F32)
        return total


class GainSum:
    def __init__(self, links, bufs):
        self.links = links
        self.own, self.got1, self.half, self.got2, self.part, self.got3 = bufs

    def first(self):
        self.copies = [self.links.start(self.own, self.got1, self.links.partner())]

    def second(self):
        k = self.links
        wait_all(self.copies)
        self.half[...] = self.own[...] + self.got1[...]
        self.copies = [
            k.start(self.half, self.got2.at[d - 1], k.device(0, 2 * d)) for d in range(1, k.chips)
        ]

    def third(self):
        k = self.links
        wait_all(self.copies)
        total = self.half[...]
        for d in range(1, k.chips):
            total = total + self.got2[d - 1]
        self.part[...] = total
        self.copies = [k.start(self.part, self.got3.at[d - 1], k.device(d, 0)) for d in range(1, k.nr)]

    def finish(self):
        wait_all(self.copies)
        total = self.part[...]
        for d in range(1, self.links.nr):
            total = total + self.got3[d - 1]
        return total


def store_parts(parts, value, offset):
    _, chips, nr, depth, _ = parts.shape
    width = value.shape[1]
    for r in range(nr):
        for x in range(chips):
            for core in range(2):
                i = (r * chips + x) * 2 + core
                piece = value[i * depth : (i + 1) * depth]
                parts[core, x, r, :, offset : offset + width] = piece.astype(BF16)


def fill_side(scratch, tile, margin):
    scratch[...] = jnp.zeros_like(scratch)
    for r in range(tile.shape[0]):
        scratch[r * margin : (r + 1) * margin, :] = tile[r, :margin, :]


def put_pieces(idx, source, row_ref, col_ref):
    got = select(idx[...], source)
    row_ref[...] = got[: row_ref.shape[0]]
    col_ref[...] = got[row_ref.shape[0] :]


def lanes_of(width, g):
    return [slice(t * width + g * LANES, t * width + (g + 1) * LANES) for t in range(3)]


def shifts_of(rows, cols, rows3, cols3):
    pitch3 = pitch_of(cols3)
    return (
        Shift(rows, cols, MARGIN, False),
        Shift(rows3, cols3, MARGIN, False, pitch3),
        Shift(rows, cols, NEAR, True),
        Shift(rows3, cols3, MARGIN, False, pitch3),
        Shift(rows3, cols3, MARGIN, True),
        Shift(rows, cols, NEAR, False),
        Shift(rows, cols, MARGIN, True),
        Shift(rows3, cols3, MARGIN, True),
    )


class Pick:
    def __init__(self, idx, local, halo):
        base, extra = local.shape[0], sum(h.shape[0] for h in halo)
        self.part = dot(one_hot(idx, base), local)
        self.hot = one_hot(idx - base, extra)
        self.halo = halo

    def finish(self, flying, at=slice(None)):
        wait_all(flying)
        rest = jnp.concatenate([h[...] for h in self.halo], axis=0)
        return (self.part[at] + dot(self.hot[at], rest)).astype(BF16)


def early_windows(rows, cols, margin):
    if 2 * WIN + margin > rows + WIN:
        return 0
    return (cols - margin) // WIN


def whole_kernel(code_sizes, in_names, out_names, scratch_names, *refs):
    b = Bag()
    for name, ref in zip(in_names + out_names + scratch_names, refs, strict=True):
        setattr(b, name, ref)
    links = Links(b.send, b.recv)
    links.greet()
    at = 0
    for name, size in code_sizes.items():
        setattr(b, name, b.codes.at[at : at + size])
        at += size
    loads = {}
    for n, name in enumerate(LATE):
        kept = getattr(b, "v_" + name)
        loads[name] = Load(pltpu.make_async_copy(getattr(b, name), kept, b.loaded.at[n]))
        setattr(b, name, kept)
    rows, cols, narrow = b.tok.shape
    rows3, cols3, wide = b.cot.shape
    pitch, pitch3 = pitch_of(cols), pitch_of(cols3)
    red3 = Reduction(links, BF16, b.g3, [getattr(b, f"g3_{i}") for i in range(5)])
    redm = Reduction(links, BF16, b.gm, [getattr(b, f"gm_{i}") for i in range(5)], True)
    red2 = Reduction(links, BF16, b.g2, [getattr(b, f"g2_{i}") for i in range(5)], True)
    redg = GainSum(links, [getattr(b, f"gg_{i}") for i in range(6)])
    ways = shifts_of(rows, cols, rows3, cols3)
    halos = [[getattr(b, f"h{n}_{i}") for i in range(3)] for n in range(len(ways))]
    row_of = [getattr(b, f"row{n}") if hasattr(b, f"row{n}") else None for n in range(len(ways))]
    col_of = [getattr(b, f"col{n}") for n in range(len(ways))]
    masks = head_masks()
    s0, s1, s2, s3 = (b.shifts[i] for i in range(4))
    e0 = jnp.minimum(s0 - (s0 & 1), 2 * s2)
    e1 = jnp.minimum(s1 - (s1 & 1), 2 * s3)
    t0, t1 = s0 - e0, s1 - e1
    d0, d1 = s2 - (e0 >> 1), s3 - (e1 >> 1)
    quads, n2, n3 = b.quad.shape[0], b.win2.shape[0], b.win3.shape[0]
    base, base3 = b.toks.shape[0], rows3 * pitch3
    as_toks = lambda h, w: h * cols + w
    as_grid3 = lambda h, w: h * pitch3 + w
    as_quad = lambda h, w: quad_index(h, w, rows, cols)
    as_win = lambda h, w: win_index(h, w, cols)
    as_win3 = lambda h, w: win_index(h, w, cols3)

    def exchange(n, row=None):
        row = row_of[n] if row is None else row
        return links.exchange(ways[n], row, col_of[n], halos[n])

    if base > rows * cols:
        b.toks[rows * cols :, :] = jnp.zeros((base - rows * cols, narrow), BF16)
    fill_tile(b.toks, b.tok, cols)
    fill_side(b.col0, b.tok, MARGIN)
    b.cots[...] = jnp.zeros_like(b.cots)
    fill_tile(b.cots, b.cot, pitch3)
    fill_side(b.col1, b.cot, MARGIN)
    links.barrier()
    flying = exchange(0, b.toks.at[0 : ways[0].row])
    flying_c = exchange(1, b.cots.at[0 : ways[1].row])

    pick = Pick(ways[0].index(b.win2[...], s0, s1, as_toks, base), b.toks[...], halos[0])
    place2 = (rows, cols, links.row, links.col, s0, s1)
    place3 = (rows3, cols3, links.row, links.col, s2, s3)
    b.lc2[...] = window_labels(b.win2[:, :SLOT], *place2)
    b.lr2[...] = window_labels(b.rwin2[...], *place2)
    b.lc3[...] = window_labels(b.win3[:, :SLOT], *place3)
    b.lr3[...] = window_labels(b.rwin3[...], *place3)
    early = early_windows(rows, cols, MARGIN)
    for half in (range(early), range(early, n2 // SLOT)):
        part = slice(half.start * SLOT, half.stop * SLOT)
        tok2 = pick.finish(flying, part) if half.start else pick.part[part].astype(BF16)
        b.tok2[part] = tok2
        hat, _ = norm_parts(tok2.astype(F32))
        b.rolled[part] = (hat * b.gain2[...]).astype(BF16)
        if half.start == 0:
            loads["qkv2"].wait()
        b.packed[part] = dot(b.rolled[part], b.qkv2[...]).astype(BF16)
        for w in half:
            bias = window_bias(b.lc2, b.lr2, w)
            at = slice(w * SLOT, (w + 1) * SLOT)
            for g in range(narrow // LANES):
                lanes = lanes_of(narrow, g)
                qs = stack_heads(b.packed[at, lanes[0]], masks)
                weights = soft(qs, b.packed[at, lanes[1]], bias)
                b.kept[w * (narrow // LANES) + g] = weights
                wb = weights.astype(BF16)
                b.mixed[at, lanes[0]] = pick_heads(dot(wb, b.packed[at, lanes[2]])).astype(BF16)
    loads["proj2"].wait()
    win = dot(b.mixed[...], b.proj2[...]).astype(BF16)
    section = (b.tok2[...].astype(F32) + win.astype(F32)).astype(BF16)
    put_pieces(b.idx2, section, b.row2, b.col2)
    flying = exchange(2)

    pick = Pick(ways[2].index(b.quad[...], t0, t1, as_win, n2), section, halos[2])
    pick_c = Pick(ways[1].index(b.win3[...], s2, s3, as_grid3, base3), b.cots[...], halos[1])
    section = pick.finish(flying)
    t3 = rows3 * pitch3
    joined = jnp.concatenate([section[k * t3 : (k + 1) * t3] for k in range(4)], axis=1)
    b.joined[...] = joined
    hat, _ = norm_parts(joined.astype(F32))
    b.mnorm[...] = (hat * b.gainm[...]).astype(BF16)
    loads["weight"].wait()
    merged = dot(b.mnorm[...], b.weight[...]).astype(BF16)
    b.merged[...] = merged
    b.col3[...] = jnp.zeros_like(b.col3)
    for r in range(rows3):
        b.col3[r * MARGIN : (r + 1) * MARGIN, :] = merged[r * pitch3 : r * pitch3 + MARGIN]
    flying = exchange(3, b.merged.at[0 : ways[3].row])

    pick = Pick(ways[3].index(b.win3[...], d0, d1, as_grid3, base3), merged, halos[3])
    b.dproj3[...] = pick_c.finish(flying_c)
    loads["proj3"].wait()
    dmixed = dot_nt(b.dproj3[...], b.proj3[...]).astype(BF16)
    merged3 = pick.finish(flying)
    b.merged3[...] = merged3
    hat, _ = norm_parts(merged3.astype(F32))
    rolled3 = (hat * b.gain3[...]).astype(BF16)
    b.rolled3[...] = rolled3
    loads["qkv3"].wait()
    b.packed3[...] = dot(rolled3, b.qkv3[...]).astype(BF16)
    for w in range(b.lr3.shape[0]):
        bias = window_bias(b.lc3, b.lr3, w)
        at = slice(w * SLOT, (w + 1) * SLOT)
        for g in range(wide // LANES):
            lanes = lanes_of(wide, g)
            qs = stack_heads(b.packed3[at, lanes[0]], masks)
            k, v = b.packed3[at, lanes[1]], b.packed3[at, lanes[2]]
            weights = soft(qs, k, bias)
            wb = weights.astype(BF16)
            b.mixed3[at, lanes[0]] = pick_heads(dot(wb, v)).astype(BF16)
            back = unit_back(qs, k, v, weights, wb, dmixed[at, lanes[0]], masks)
            for t in range(3):
                b.dpacked3[at, lanes[t]] = back[t]
    drolled3 = dot_nt(b.dpacked3[...], b.qkv3[...]).astype(BF16)
    hat, inv = norm_parts(b.merged3[...].astype(F32))
    dmerged3, grad3 = norm_back(hat, inv, b.gain3[...], drolled3.astype(F32))
    dmerged3 = b.dproj3[...] + dmerged3
    put_pieces(b.idx4, dmerged3, b.row4, b.col4)
    flying = exchange(4)
    store_parts(b.g3, dot_tn(b.rolled3[...], b.dpacked3[...]), 0)
    store_parts(b.g3, dot_tn(b.mixed3[...], b.dproj3[...]), 3 * wide)
    red3.first_away()
    red3.first_own()
    proj = dot(b.mixed3[...], b.proj3[...]).astype(BF16)
    out3 = (b.merged3[...].astype(F32) + proj.astype(F32)).astype(BF16)
    put_pieces(b.idx7, out3, b.row7, b.col7)
    flying_o = exchange(7)
    pick_o = Pick(ways[7].index(b.grid3[...], s2, s3, as_win3, n3), out3, halos[7])
    pick = Pick(ways[4].index(b.grid3[...], d0, d1, as_win3, n3), dmerged3, halos[4])
    red3.second(1)
    hat, inv = norm_parts(b.joined[...].astype(F32))
    dmerged = pick.finish(flying)
    djn = dot_nt(dmerged, b.weight[...]).astype(BF16).astype(F32)
    djoined, gradm = norm_back(hat, inv, b.gainm[...], djn)
    b.gg_0[:, narrow : 5 * narrow] = gradm
    b.gg_0[:, 5 * narrow :] = grad3
    b.dsec[...] = jnp.concatenate(
        [djoined[:, k * narrow : (k + 1) * narrow] for k in range(4)], axis=0
    )
    put_pieces(b.idx5, b.dsec[...], b.row5, b.col5)
    flying = exchange(5)
    store_parts(b.gm, dot_tn(b.mnorm[...], dmerged), 0)
    redm.first_away()
    redm.first_own()
    red3.second()
    pick = Pick(ways[5].index(b.win2[...], t0, t1, as_quad, quads), b.dsec[...], halos[5])
    early = early_windows(rows, cols, NEAR)
    halves = [range(early), range(early, n2 // SLOT)]
    for half in halves:
        part = slice(half.start * SLOT, half.stop * SLOT)
        if half.start == 0:
            b.dsec2[part] = pick.part[part].astype(BF16)
        else:
            b.dsec2[part] = pick.finish(flying, part)
        dmixed = dot_nt(b.dsec2[part], b.proj2[...]).astype(BF16)
        for w in half:
            at = slice(w * SLOT, (w + 1) * SLOT)
            here = slice(at.start - part.start, at.stop - part.start)
            for g in range(narrow // LANES):
                lanes = lanes_of(narrow, g)
                qs = stack_heads(b.packed[at, lanes[0]], masks)
                k, v = b.packed[at, lanes[1]], b.packed[at, lanes[2]]
                weights = b.kept[w * (narrow // LANES) + g]
                back = unit_back(
                    qs, k, v, weights, weights.astype(BF16), dmixed[here, lanes[0]], masks
                )
                for t in range(3):
                    b.dpacked[at, lanes[t]] = back[t]
            if w == 0:
                redm.second()
            if w in (2, 3, 4):
                red3.third(1)
    drolled = dot_nt(b.dpacked[...], b.qkv2[...]).astype(BF16)
    hat, inv = norm_parts(b.tok2[...].astype(F32))
    dtok2, grad2 = norm_back(hat, inv, b.gain2[...], drolled.astype(F32))
    dtok2 = b.dsec2[...] + dtok2
    put_pieces(b.idx6, dtok2, b.row6, b.col6)
    flying = exchange(6)
    b.gg_0[:, :narrow] = grad2
    redg.first()
    store_parts(b.g2, dot_tn(b.rolled[...], b.dpacked[...]), 0)
    store_parts(b.g2, dot_tn(b.mixed[...], b.dsec2[...]), 3 * narrow)
    redg.second()
    red2.first_away()
    red2.first_own()
    red3.third()
    total = pick_o.finish(flying_o)
    for r in range(rows3):
        b.out[r] = total[r * pitch3 : r * pitch3 + cols3]
    red2.second()
    redm.third()
    pick = Pick(ways[6].index(b.nat[...], s0, s1, as_win, n2), dtok2, halos[6])
    total = pick.finish(flying)
    for r in range(rows):
        b.dtok[r] = total[r * pitch : r * pitch + cols]
    redg.third()
    red2.third()
    b.sum3[...] = red3.finish().astype(BF16)
    b.summ[...] = redm.finish().astype(BF16)
    b.sum2[...] = red2.finish().astype(BF16)
    b.gains[...] = redg.finish()


def finish_kernel(out, dtok, gains, sum3, summ, sum2, o_out, o_dtok, o_gains, *rest):
    o_out[...] = out[...]
    o_dtok[...] = dtok[...]
    for j in range(o_gains.shape[0]):
        o_gains[j : j + 1, :] = gains[:, j * LANES : (j + 1) * LANES]
    flats, rooms = rest[: len(rest) // 2], rest[len(rest) // 2 :]
    wide, narrow = sum3.shape[1] // 4, sum2.shape[1] // 4
    views = (
        (sum2, 0, 3 * narrow), (sum2, 3 * narrow, narrow), (summ, 0, wide),
        (sum3, 0, 3 * wide), (sum3, 3 * wide, wide),
    )
    for (source, offset, width), flat, room in zip(views, flats, rooms, strict=True):
        steps = width // LANES
        for j in range(steps):
            piece = source[:, offset + j * LANES : offset + (j + 1) * LANES]
            room[pl.ds(j, source.shape[0], stride=steps), :] = piece.astype(F32)
        flat[...] = room[...].astype(BF16)


def on_device(
    tokens, cotangent, shifts, norm2_gain, qkv2, proj2, merge_gain, merge_weight, norm3_gain,
    qkv3, proj3,
):
    rows, cols, narrow = tokens.shape
    wide = qkv3.shape[0]
    rows3, cols3 = rows // 2, cols // 2
    pitch, pitch3 = pitch_of(cols), pitch_of(cols3)
    base, base3 = padded(rows * cols), rows3 * pitch3
    win2, win3 = window_tokens(rows, cols), window_tokens(rows3, cols3)
    n2, n3 = len(win2[0]), len(win3[0])
    quad = quad_tokens(rows, cols)
    nat = grid_tokens(rows, cols, pitch)
    grid3 = grid_tokens(rows3, cols3, pitch3)
    as_quad = lambda h, w: quad_index(h, w, rows, cols)
    as_win = lambda h, w: win_index(h, w, cols)
    as_win3 = lambda h, w: win_index(h, w, cols3)
    ways = shifts_of(rows, cols, rows3, cols3)
    gain2, gainm, gain3 = (g.reshape(1, -1) for g in (norm2_gain, merge_gain, norm3_gain))
    nr, nc = lax.axis_size("rows"), lax.axis_size("cols")
    chips = nc // 2
    quads, gains = len(quad[0]), 5 * narrow + wide
    codes = dict(
        win2=coded(win2), win3=coded(win3), quad=coded(quad), nat=coded(nat), grid3=coded(grid3),
        idx2=ways[2].pieces(as_win), idx4=ways[4].pieces(as_win3), idx5=ways[5].pieces(as_quad),
        idx6=ways[6].pieces(as_win), idx7=ways[7].pieces(as_win3),
    )
    inputs = dict(
        tok=tokens, cot=cotangent, shifts=shifts, codes=np.concatenate(list(codes.values())),
        rwin2=coded(win2)[:, 0].reshape(-1, SLOT), rwin3=coded(win3)[:, 0].reshape(-1, SLOT),
        gain2=gain2, gainm=gainm, gain3=gain3, qkv2=qkv2, proj2=proj2,
        weight=merge_weight, qkv3=qkv3, proj3=proj3,
    )
    m3, mm, m2 = wide // (nr * nc), 4 * narrow // (nr * nc), narrow // (nr * nc)
    outs = dict(
        out=(cotangent.shape, BF16),
        dtok=(tokens.shape, BF16),
        gains=((1, gains), F32),
        sum3=((m3, 4 * wide), BF16),
        summ=((mm, wide), BF16),
        sum2=((m2, 4 * narrow), BF16),
    )
    scratch = dict(
        toks=((base, narrow), BF16), cots=((base3, wide), BF16),
        tok2=((n2, narrow), BF16),
        rolled=((n2, narrow), BF16), packed=((n2, 3 * narrow), BF16), mixed=((n2, narrow), BF16),
        joined=((base3, 4 * narrow), BF16), mnorm=((base3, 4 * narrow), BF16),
        merged=((base3, wide), BF16), merged3=((n3, wide), BF16), rolled3=((n3, wide), BF16),
        dproj3=((n3, wide), BF16),
        packed3=((n3, 3 * wide), BF16), mixed3=((n3, wide), BF16),
        dpacked3=((n3, 3 * wide), BF16), dsec=((quads, narrow), BF16),
        dsec2=((n2, narrow), BF16), dpacked=((n2, 3 * narrow), BF16),
    )
    kept = (n2 // SLOT * (narrow // LANES), PACK * SLOT, SLOT)
    ints = dict(lc2=(n2, SLOT), lr2=(n2 // SLOT, SLOT), lc3=(n3, SLOT), lr3=(n3 // SLOT, SLOT))
    scratch |= {name: (shape, jnp.int32) for name, shape in ints.items()}
    scratch["kept"] = (kept, F32)
    for name in LATE:
        scratch["v_" + name] = (inputs[name].shape, inputs[name].dtype)
    copies = len(ways) * 3
    for n, way in enumerate(ways):
        width = narrow if way.rows == rows else wide
        if n not in (0, 1, 3):
            scratch[f"row{n}"] = ((way.row, width), BF16)
        scratch[f"col{n}"] = ((way.col, width), BF16)
        for i, size in enumerate(way.sizes()):
            scratch[f"h{n}_{i}"] = ((size, width), BF16)
    for name, shape in (("g3", (m3, 4 * wide)), ("gm", (mm, wide)), ("g2", (m2, 4 * narrow))):
        scratch[name] = ((2, chips, nr) + shape, BF16)
        for i, lead in enumerate(
            ((chips, nr), (chips, nr), (max(chips - 1, 1), nr), (nr,), (max(nr - 1, 1),))
        ):
            scratch[f"{name}_{i}"] = (lead + shape, BF16)
        copies += chips + (chips - 1) * nr + nr - 1
    for i, lead in enumerate(((), (), (), (max(chips - 1, 1),), (), (max(nr - 1, 1),))):
        scratch[f"gg_{i}"] = (lead + (1, gains), F32)
    copies += chips + nr - 1
    spaces = [pltpu.VMEM(s, d) for s, d in scratch.values()]
    spaces += [pltpu.SemaphoreType.DMA((n,)) for n in (copies, copies, len(LATE))]
    results = pl.pallas_call(
        functools.partial(
            whole_kernel, {k: len(v) for k, v in codes.items()}, list(inputs), list(outs), list(scratch) + ["send", "recv", "loaded"]
        ),
        out_shape=[jax.ShapeDtypeStruct(s, d) for s, d in outs.values()],
        in_specs=[
            pl.BlockSpec(
                memory_space=pltpu.SMEM if name == "shifts" else pl.ANY if name in LATE else pltpu.VMEM
            )
            for name in inputs
        ],
        out_specs=[pl.BlockSpec(memory_space=pltpu.VMEM)] * len(outs),
        scratch_shapes=spaces,
        compiler_params=pltpu.CompilerParams(
            collective_id=0, has_side_effects=True, vmem_limit_bytes=60 * 2**20
        ),
        name="block",
    )(*inputs.values())
    flats = [
        (m * width // LANES, LANES)
        for m, width in (
            (m2, 3 * narrow), (m2, narrow), (mm, wide), (m3, 3 * wide), (m3, wide)
        )
    ]
    final = pl.pallas_call(
        finish_kernel,
        out_shape=[
            jax.ShapeDtypeStruct(cotangent.shape, BF16),
            jax.ShapeDtypeStruct(tokens.shape, BF16),
            jax.ShapeDtypeStruct((gains // LANES, LANES), F32),
        ]
        + [jax.ShapeDtypeStruct(shape, BF16) for shape in flats],
        scratch_shapes=[pltpu.VMEM(shape, F32) for shape in flats],
        name="finish",
    )(*results)
    return tuple(final[:2]) + tuple(x.reshape(-1) for x in final[2:])


def solution(mesh):
    tile = P(("groups", "rows"), "cols", None)
    spread = P(("groups", "rows", "cols"))
    return jax.shard_map(
        on_device,
        mesh=mesh,
        in_specs=(tile, tile) + (P(),) * 9,
        out_specs=(tile, tile, P("groups")) + (spread,) * 5,
        check_vma=False,
    )
```

```python
import functools

import jax
import jax.numpy as jnp
import numpy as np
from jax import lax
from jax.experimental import pallas as pl
from jax.experimental.pallas import tpu as pltpu
from jax.sharding import PartitionSpec as P

HEAD = 32
WIN = 7
MARGIN = WIN - 1
NEAR = 4
SLOT = 64
LANES = 128
EPSILON = 1e-05
MASKED = -100.0
F32 = jnp.float32
BF16 = jnp.bfloat16


def pitch_of(count):
    return -(-count // 16) * 16


def window_tokens(rows, cols):
    h, w, ok = [], [], []
    for wr in range(rows // WIN):
        for wc in range(cols // WIN):
            for t in range(SLOT):
                good = t < WIN * WIN
                h.append(wr * WIN + t // WIN if good else 0)
                w.append(wc * WIN + t % WIN if good else 0)
                ok.append(good)
    return np.array(h, np.int32), np.array(w, np.int32), np.array(ok)


def grid_tokens(rows, cols, pitch):
    h = np.repeat(np.arange(rows, dtype=np.int32), pitch)
    w = np.tile(np.arange(pitch, dtype=np.int32), rows)
    ok = w < cols
    return h, np.where(ok, w, 0).astype(np.int32), ok


def quad_tokens(rows, cols):
    a, b, ok = grid_tokens(rows // 2, cols // 2, pitch_of(cols // 2))
    h = np.concatenate([2 * a + (k & 1) for k in range(4)])
    w = np.concatenate([2 * b + (k >> 1) for k in range(4)])
    return h, w, np.tile(ok, 4)


def by_window(x):
    return (x * 9363) >> 16


def win_index(h, w, cols):
    hq, wq = by_window(h), by_window(w)
    return (hq * (cols // WIN) + wq) * SLOT + (h - hq * WIN) * WIN + w - wq * WIN


def quad_index(h, w, rows, cols):
    pitch = pitch_of(cols // 2)
    return ((h & 1) + 2 * (w & 1)) * ((rows // 2) * pitch) + (h >> 1) * pitch + (w >> 1)


def spread(values):
    return np.repeat(values.astype(np.int32).reshape(-1, 1), LANES, axis=1)


def coded(tokens):
    h, w, ok = tokens
    return spread(np.where(ok, h * 4096 + w, -1))


def decoded(code):
    return code >> 12, code & 4095, code >= 0


def padded(count):
    return -(-count // 16) * 16


class Shift:
    def __init__(self, rows, cols, margin, behind, pitch=None):
        self.rows, self.cols, self.margin, self.behind = rows, cols, margin, behind
        self.pitch = pitch or cols
        self.row = padded(margin * self.pitch)
        self.col = padded(rows * margin)
        self.first = (rows - margin) * margin // 16 * 16 if behind else 0
        self.corner = (self.col if behind else padded(margin * margin)) - self.first
        self.by = 1 if behind else -1
        self.extra = self.row + self.col + self.corner

    def sizes(self):
        return self.row, self.col, self.corner

    def index(self, code, by_rows, by_cols, inner, base):
        h, w, ok = decoded(code)
        m, rows, cols = self.margin, self.rows, self.cols
        if self.behind:
            h2, w2 = h - by_rows, w - by_cols
            local = inner(jnp.maximum(h2, 0), jnp.maximum(w2, 0))
            out_row, out_col = h2 < 0, w2 < 0
            r, c = h2 + m, w2 + m
            corner = (h2 + rows) * m - self.first + c
        else:
            h2, w2 = h + by_rows, w + by_cols
            local = inner(jnp.minimum(h2, rows - 1), jnp.minimum(w2, cols - 1))
            out_row, out_col = h2 >= rows, w2 >= cols
            r, c = h2 - rows, w2 - cols
            corner = r * m + c
        row = base + r * self.pitch + w2
        side = base + self.row + h2 * m + c
        corner = base + self.row + self.col + corner
        got = jnp.where(
            out_row, jnp.where(out_col, corner, row), jnp.where(out_col, side, local)
        )
        return jnp.where(ok, got, -1)

    def pieces(self, inner):
        m = self.margin
        top = self.rows - m if self.behind else 0
        left = self.cols - m if self.behind else 0
        parts = []
        for count, wide, pitch, h0, w0, size in (
            (m, self.cols, self.pitch, top, 0, self.row),
            (self.rows, m, m, 0, left, self.col),
        ):
            h, w, ok = grid_tokens(count, wide, pitch)
            got = np.where(ok, inner(h + h0, w + w0), -1)
            parts.append(np.pad(got, (0, size - len(got)), constant_values=-1))
        return spread(np.concatenate(parts))


def window_labels(code, rows, cols, axis_row, axis_col, shift_rows, shift_cols):
    h, w, ok = decoded(code)
    height = rows * lax.axis_size("rows")
    breadth = cols * lax.axis_size("cols")
    gh = axis_row * rows + h
    gw = axis_col * cols + w
    lh = jnp.where(gh < height - WIN, 0, jnp.where(gh < height - shift_rows, 1, 2))
    lw = jnp.where(gw < breadth - WIN, 0, jnp.where(gw < breadth - shift_cols, 1, 2))
    return jnp.where(ok, lh * 3 + lw, -1)


def dot(a, b):
    return jnp.dot(a, b, preferred_element_type=F32)


def dot_nt(a, b):
    return lax.dot_general(a, b, (((1,), (1,)), ((), ())), preferred_element_type=F32)


def dot_tn(a, b):
    return lax.dot_general(a, b, (((0,), (0,)), ((), ())), preferred_element_type=F32)


def one_hot(idx, count):
    lane = lax.broadcasted_iota(jnp.int32, (1, LANES), 1)
    parts = []
    for start in range(0, count, LANES):
        wide = min(LANES, count - start)
        parts.append(jnp.where(idx[:, :wide] == lane[:, :wide] + start, 1.0, 0.0).astype(BF16))
    return jnp.concatenate(parts, axis=1)


def picked(hot, source):
    return dot(hot, source).astype(BF16)


def select(idx, source):
    return picked(one_hot(idx, source.shape[0]), source)


def norm_parts(x):
    centred = x - jnp.mean(x, axis=-1, keepdims=True)
    inverse = lax.rsqrt(jnp.mean(centred * centred, axis=-1, keepdims=True) + EPSILON)
    return centred * inverse, inverse


def norm_back(hat, inverse, gain, dy):
    grad_gain = jnp.sum(dy * hat, axis=0, keepdims=True)
    t = dy * gain
    dx = inverse * (
        t
        - jnp.mean(t, axis=-1, keepdims=True)
        - hat * jnp.mean(t * hat, axis=-1, keepdims=True)
    )
    return dx.astype(BF16), grad_gain


PACK = LANES // HEAD


def head_masks():
    lane = lax.broadcasted_iota(jnp.int32, (1, LANES), 1) // HEAD
    return [jnp.where(lane == h, 1.0, 0.0).astype(BF16) for h in range(PACK)]


def stack_heads(x, masks):
    return jnp.concatenate([x * m for m in masks], axis=0)


def pick_heads(o):
    lane = lax.broadcasted_iota(jnp.int32, (SLOT, LANES), 1) // HEAD
    out = o[:SLOT]
    for h in range(1, PACK):
        out = jnp.where(lane == h, o[h * SLOT : (h + 1) * SLOT], out)
    return out


def window_bias(lc_ref, lr_ref, w):
    lc = lc_ref[w * SLOT : (w + 1) * SLOT, :]
    lr = lr_ref[w : w + 1, :]
    bias = jnp.where((lc == lr) | (lc < 0), 0.0, MASKED)
    bias = jnp.where(lr < 0, -1e30, bias)
    return jnp.concatenate([bias] * PACK, axis=0)


def soft(qs, k, bias):
    raised = jnp.exp(dot_nt(qs, k) * HEAD ** (-0.5) + bias)
    return raised * (1.0 / jnp.sum(raised, axis=-1, keepdims=True))


def unit_back(qs, k, v, weights, wb, dm, masks):
    dms = stack_heads(dm, masks)
    dw = dot_nt(dms, v).astype(BF16).astype(F32)
    ds = weights * (dw - jnp.sum(dw * weights, axis=-1, keepdims=True))
    ds = (ds * HEAD ** (-0.5)).astype(BF16)
    dq = pick_heads(dot(ds, k))
    dk = dot_tn(ds, qs)
    dv = dot_tn(wb, dms)
    return dq.astype(BF16), dk.astype(BF16), dv.astype(BF16)


def fill_tile(scratch, tile, pitch):
    count, wide, _ = tile.shape
    for r in range(count):
        scratch[r * pitch : r * pitch + wide, :] = tile[r]


LATE = ("qkv2", "proj2", "weight", "proj3", "qkv3", )


class Load:
    def __init__(self, copy):
        self.copy, self.flying = copy, True
        copy.start()

    def wait(self):
        if self.flying:
            self.copy.wait()
        self.flying = False


class Bag:
    pass


MESH = pl.DeviceIdType.MESH


class Links:
    def __init__(self, send, recv):
        self.send, self.recv, self.used = send, recv, 0
        self.group = lax.axis_index("groups")
        self.row, self.col = lax.axis_index("rows"), lax.axis_index("cols")
        self.nr, self.nc = lax.axis_size("rows"), lax.axis_size("cols")
        self.core, self.chip = lax.rem(self.col, 2), self.col // 2
        self.chips = self.nc // 2

    def device(self, dr, dc):
        row = lax.rem(self.row + dr + self.nr, self.nr)
        col = lax.rem(self.col + dc + self.nc, self.nc)
        return (self.group, row, col)

    def partner(self):
        return (self.group, self.row, self.chip * 2 + 1 - self.core)

    def greet(self):
        offsets = {(d, 0) for d in range(1, self.nr)} | {(0, d) for d in range(1, self.nc)}
        offsets |= {(1, 1), (self.nr - 1, self.nc - 1)}
        self.greeted = len(offsets)
        sem = pltpu.get_barrier_semaphore()
        for dr, dc in sorted(offsets):
            pl.semaphore_signal(sem, inc=1, device_id=self.device(dr, dc), device_id_type=MESH)

    def barrier(self):
        pl.semaphore_wait(pltpu.get_barrier_semaphore(), self.greeted)

    def start(self, source, target, device):
        copy = pltpu.make_async_remote_copy(
            src_ref=source,
            dst_ref=target,
            send_sem=self.send.at[self.used],
            recv_sem=self.recv.at[self.used],
            device_id=device,
            device_id_type=MESH,
        )
        self.used += 1
        copy.start()
        return copy

    def exchange(self, shift, row, col, halo):
        by = shift.by
        corner = col.at[shift.first : shift.first + shift.corner]
        return [
            self.start(corner, halo[2], self.device(by, by)),
            self.start(row, halo[0], self.device(by, 0)),
            self.start(col, halo[1], self.device(0, by)),
        ]


def wait_all(copies):
    for copy in copies:
        copy.wait()


class Reduction:
    def __init__(self, links, kind, parts, bufs, whole=False):
        self.links, self.kind, self.parts, self.whole = links, kind, parts, whole
        self.got1, self.half, self.got2, self.part, self.got3 = bufs
        self.arriving, self.sent, self.copies, self.step = {}, 1, [], 1


    def start_first(self, d):
        k = self.links
        x = lax.rem(k.chip + d, k.chips)
        return k.start(self.parts.at[1 - k.core, x], self.got1.at[x], k.partner())

    def first_away(self):
        k = self.links
        if self.whole:
            self.own = k.start(self.parts.at[1 - k.core], self.got1, k.partner())
            self.away = [self.own]
        else:
            self.away = [self.start_first(d) for d in range(1, k.chips)]

    def first_own(self):
        if not self.whole:
            self.own = self.start_first(0)

    def both_cores(self, x, r):
        return self.parts[self.links.core, x, r].astype(F32) + self.got1[x, r].astype(F32)

    def second(self, steps=99):
        k = self.links
        if self.whole:
            wait_all(self.away)
            for d in range(1, k.chips):
                x = lax.rem(k.chip + d, k.chips)
                for r in range(k.nr):
                    self.half[x, r] = self.both_cores(x, r).astype(self.kind)
                self.arriving[1, d] = k.start(
                    self.half.at[x], self.got2.at[d - 1], k.device(0, 2 * d)
                )
            return
        if not self.arriving:
            wait_all(self.away)
        for e in range(self.sent, min(self.sent + steps, k.nr + 1)):
            r = lax.rem(k.row + e, k.nr)
            for d in range(1, k.chips):
                x = lax.rem(k.chip + d, k.chips)
                self.half[x, r] = self.both_cores(x, r).astype(self.kind)
                self.arriving[e, d] = k.start(
                    self.half.at[x, r], self.got2.at[d - 1, r], k.device(0, 2 * d)
                )
        self.sent += steps

    def third(self, steps=None):
        k = self.links
        if self.step == 1 and not self.whole:
            self.own.wait()
        stop = k.nr + 1 if steps is None else min(self.step + steps, k.nr + 1)
        for e in range(self.step, stop):
            r = lax.rem(k.row + e, k.nr)
            total = self.both_cores(k.chip, r)
            for d in range(1, k.chips):
                if (e, d) in self.arriving:
                    self.arriving[e, d].wait()
                total = total + self.got2[d - 1, r].astype(F32)
            self.part[r] = total.astype(self.kind)
            if e < k.nr:
                self.copies.append(k.start(self.part.at[r], self.got3.at[e - 1], k.device(e, 0)))
        self.step = stop

    def finish(self):
        k = self.links
        wait_all(self.copies)
        total = self.part[k.row].astype(F32)
        for d in range(1, k.nr):
            total = total + self.got3[d - 1].astype(F32)
        return total


class GainSum:
    def __init__(self, links, bufs):
        self.links = links
        self.own, self.got1, self.half, self.got2, self.part, self.got3 = bufs

    def first(self):
        self.copies = [self.links.start(self.own, self.got1, self.links.partner())]

    def second(self):
        k = self.links
        wait_all(self.copies)
        self.half[...] = self.own[...] + self.got1[...]
        self.copies = [
            k.start(self.half, self.got2.at[d - 1], k.device(0, 2 * d)) for d in range(1, k.chips)
        ]

    def third(self):
        k = self.links
        wait_all(self.copies)
        total = self.half[...]
        for d in range(1, k.chips):
            total = total + self.got2[d - 1]
        self.part[...] = total
        self.copies = [k.start(self.part, self.got3.at[d - 1], k.device(d, 0)) for d in range(1, k.nr)]

    def finish(self):
        wait_all(self.copies)
        total = self.part[...]
        for d in range(1, self.links.nr):
            total = total + self.got3[d - 1]
        return total


def store_parts(parts, value, offset):
    _, chips, nr, depth, _ = parts.shape
    width = value.shape[1]
    for r in range(nr):
        for x in range(chips):
            for core in range(2):
                i = (r * chips + x) * 2 + core
                piece = value[i * depth : (i + 1) * depth]
                parts[core, x, r, :, offset : offset + width] = piece.astype(BF16)


def fill_side(scratch, tile, margin):
    scratch[...] = jnp.zeros_like(scratch)
    for r in range(tile.shape[0]):
        scratch[r * margin : (r + 1) * margin, :] = tile[r, :margin, :]


def put_pieces(idx, source, row_ref, col_ref):
    got = select(idx[...], source)
    row_ref[...] = got[: row_ref.shape[0]]
    col_ref[...] = got[row_ref.shape[0] :]


def lanes_of(width, g):
    return [slice(t * width + g * LANES, t * width + (g + 1) * LANES) for t in range(3)]


def shifts_of(rows, cols, rows3, cols3):
    pitch3 = pitch_of(cols3)
    return (
        Shift(rows, cols, MARGIN, False),
        Shift(rows3, cols3, MARGIN, False, pitch3),
        Shift(rows, cols, NEAR, True),
        Shift(rows3, cols3, MARGIN, False, pitch3),
        Shift(rows3, cols3, MARGIN, True),
        Shift(rows, cols, NEAR, False),
        Shift(rows, cols, MARGIN, True),
        Shift(rows3, cols3, MARGIN, True),
    )


class Pick:
    def __init__(self, idx, local, halo):
        base, extra = local.shape[0], sum(h.shape[0] for h in halo)
        self.part = dot(one_hot(idx, base), local)
        self.hot = one_hot(idx - base, extra)
        self.halo = halo

    def finish(self, flying, at=slice(None)):
        wait_all(flying)
        rest = jnp.concatenate([h[...] for h in self.halo], axis=0)
        return (self.part[at] + dot(self.hot[at], rest)).astype(BF16)


def early_windows(rows, cols, margin):
    if 2 * WIN + margin > rows + WIN:
        return 0
    return (cols - margin) // WIN


def whole_kernel(code_sizes, in_names, out_names, scratch_names, *refs):
    b = Bag()
    for name, ref in zip(in_names + out_names + scratch_names, refs, strict=True):
        setattr(b, name, ref)
    links = Links(b.send, b.recv)
    links.greet()
    at = 0
    for name, size in code_sizes.items():
        setattr(b, name, b.codes.at[at : at + size])
        at += size
    loads = {}
    for n, name in enumerate(LATE):
        kept = getattr(b, "v_" + name)
        loads[name] = Load(pltpu.make_async_copy(getattr(b, name), kept, b.loaded.at[n]))
        setattr(b, name, kept)
    rows, cols, narrow = b.tok.shape
    rows3, cols3, wide = b.cot.shape
    pitch, pitch3 = pitch_of(cols), pitch_of(cols3)
    red3 = Reduction(links, BF16, b.g3, [getattr(b, f"g3_{i}") for i in range(5)])
    redm = Reduction(links, BF16, b.gm, [getattr(b, f"gm_{i}") for i in range(5)], True)
    red2 = Reduction(links, BF16, b.g2, [getattr(b, f"g2_{i}") for i in range(5)], True)
    redg = GainSum(links, [getattr(b, f"gg_{i}") for i in range(6)])
    ways = shifts_of(rows, cols, rows3, cols3)
    halos = [[getattr(b, f"h{n}_{i}") for i in range(3)] for n in range(len(ways))]
    row_of = [getattr(b, f"row{n}") if hasattr(b, f"row{n}") else None for n in range(len(ways))]
    col_of = [getattr(b, f"col{n}") for n in range(len(ways))]
    masks = head_masks()
    s0, s1, s2, s3 = (b.shifts[i] for i in range(4))
    e0 = jnp.minimum(s0 - (s0 & 1), 2 * s2)
    e1 = jnp.minimum(s1 - (s1 & 1), 2 * s3)
    t0, t1 = s0 - e0, s1 - e1
    d0, d1 = s2 - (e0 >> 1), s3 - (e1 >> 1)
    quads, n2, n3 = b.quad.shape[0], b.win2.shape[0], b.win3.shape[0]
    base, base3 = b.toks.shape[0], rows3 * pitch3
    as_toks = lambda h, w: h * cols + w
    as_grid3 = lambda h, w: h * pitch3 + w
    as_quad = lambda h, w: quad_index(h, w, rows, cols)
    as_win = lambda h, w: win_index(h, w, cols)
    as_win3 = lambda h, w: win_index(h, w, cols3)

    def exchange(n, row=None):
        row = row_of[n] if row is None else row
        return links.exchange(ways[n], row, col_of[n], halos[n])

    if base > rows * cols:
        b.toks[rows * cols :, :] = jnp.zeros((base - rows * cols, narrow), BF16)
    fill_tile(b.toks, b.tok, cols)
    fill_side(b.col0, b.tok, MARGIN)
    b.cots[...] = jnp.zeros_like(b.cots)
    fill_tile(b.cots, b.cot, pitch3)
    fill_side(b.col1, b.cot, MARGIN)
    links.barrier()
    flying = exchange(0, b.toks.at[0 : ways[0].row])
    flying_c = exchange(1, b.cots.at[0 : ways[1].row])

    pick = Pick(ways[0].index(b.win2[...], s0, s1, as_toks, base), b.toks[...], halos[0])
    place2 = (rows, cols, links.row, links.col, s0, s1)
    place3 = (rows3, cols3, links.row, links.col, s2, s3)
    b.lc2[...] = window_labels(b.win2[:, :SLOT], *place2)
    b.lr2[...] = window_labels(b.rwin2[...], *place2)
    b.lc3[...] = window_labels(b.win3[:, :SLOT], *place3)
    b.lr3[...] = window_labels(b.rwin3[...], *place3)
    early = early_windows(rows, cols, MARGIN)
    for half in (range(early), range(early, n2 // SLOT)):
        part = slice(half.start * SLOT, half.stop * SLOT)
        tok2 = pick.finish(flying, part) if half.start else pick.part[part].astype(BF16)
        b.tok2[part] = tok2
        hat, _ = norm_parts(tok2.astype(F32))
        b.rolled[part] = (hat * b.gain2[...]).astype(BF16)
        if half.start == 0:
            loads["qkv2"].wait()
        b.packed[part] = dot(b.rolled[part], b.qkv2[...]).astype(BF16)
        for w in half:
            bias = window_bias(b.lc2, b.lr2, w)
            at = slice(w * SLOT, (w + 1) * SLOT)
            for g in range(narrow // LANES):
                lanes = lanes_of(narrow, g)
                qs = stack_heads(b.packed[at, lanes[0]], masks)
                weights = soft(qs, b.packed[at, lanes[1]], bias)
                b.kept[w * (narrow // LANES) + g] = weights
                wb = weights.astype(BF16)
                b.mixed[at, lanes[0]] = pick_heads(dot(wb, b.packed[at, lanes[2]])).astype(BF16)
    loads["proj2"].wait()
    win = dot(b.mixed[...], b.proj2[...]).astype(BF16)
    section = (b.tok2[...].astype(F32) + win.astype(F32)).astype(BF16)
    put_pieces(b.idx2, section, b.row2, b.col2)
    flying = exchange(2)

    pick = Pick(ways[2].index(b.quad[...], t0, t1, as_win, n2), section, halos[2])
    pick_c = Pick(ways[1].index(b.win3[...], s2, s3, as_grid3, base3), b.cots[...], halos[1])
    section = pick.finish(flying)
    t3 = rows3 * pitch3
    joined = jnp.concatenate([section[k * t3 : (k + 1) * t3] for k in range(4)], axis=1)
    b.joined[...] = joined
    hat, _ = norm_parts(joined.astype(F32))
    b.mnorm[...] = (hat * b.gainm[...]).astype(BF16)
    loads["weight"].wait()
    merged = dot(b.mnorm[...], b.weight[...]).astype(BF16)
    b.merged[...] = merged
    b.col3[...] = jnp.zeros_like(b.col3)
    for r in range(rows3):
        b.col3[r * MARGIN : (r + 1) * MARGIN, :] = merged[r * pitch3 : r * pitch3 + MARGIN]
    flying = exchange(3, b.merged.at[0 : ways[3].row])

    pick = Pick(ways[3].index(b.win3[...], d0, d1, as_grid3, base3), merged, halos[3])
    b.dproj3[...] = pick_c.finish(flying_c)
    loads["proj3"].wait()
    dmixed = dot_nt(b.dproj3[...], b.proj3[...]).astype(BF16)
    merged3 = pick.finish(flying)
    b.merged3[...] = merged3
    hat, _ = norm_parts(merged3.astype(F32))
    rolled3 = (hat * b.gain3[...]).astype(BF16)
    b.rolled3[...] = rolled3
    loads["qkv3"].wait()
    b.packed3[...] = dot(rolled3, b.qkv3[...]).astype(BF16)
    for w in range(b.lr3.shape[0]):
        bias = window_bias(b.lc3, b.lr3, w)
        at = slice(w * SLOT, (w + 1) * SLOT)
        for g in range(wide // LANES):
            lanes = lanes_of(wide, g)
            qs = stack_heads(b.packed3[at, lanes[0]], masks)
            k, v = b.packed3[at, lanes[1]], b.packed3[at, lanes[2]]
            weights = soft(qs, k, bias)
            wb = weights.astype(BF16)
            b.mixed3[at, lanes[0]] = pick_heads(dot(wb, v)).astype(BF16)
            back = unit_back(qs, k, v, weights, wb, dmixed[at, lanes[0]], masks)
            for t in range(3):
                b.dpacked3[at, lanes[t]] = back[t]
    drolled3 = dot_nt(b.dpacked3[...], b.qkv3[...]).astype(BF16)
    hat, inv = norm_parts(b.merged3[...].astype(F32))
    dmerged3, grad3 = norm_back(hat, inv, b.gain3[...], drolled3.astype(F32))
    dmerged3 = b.dproj3[...] + dmerged3
    put_pieces(b.idx4, dmerged3, b.row4, b.col4)
    flying = exchange(4)
    store_parts(b.g3, dot_tn(b.rolled3[...], b.dpacked3[...]), 0)
    store_parts(b.g3, dot_tn(b.mixed3[...], b.dproj3[...]), 3 * wide)
    red3.first_away()
    red3.first_own()
    proj = dot(b.mixed3[...], b.proj3[...]).astype(BF16)
    out3 = (b.merged3[...].astype(F32) + proj.astype(F32)).astype(BF16)
    put_pieces(b.idx7, out3, b.row7, b.col7)
    flying_o = exchange(7)
    pick_o = Pick(ways[7].index(b.grid3[...], s2, s3, as_win3, n3), out3, halos[7])
    pick = Pick(ways[4].index(b.grid3[...], d0, d1, as_win3, n3), dmerged3, halos[4])
    red3.second(1)
    hat, inv = norm_parts(b.joined[...].astype(F32))
    dmerged = pick.finish(flying)
    djn = dot_nt(dmerged, b.weight[...]).astype(BF16).astype(F32)
    djoined, gradm = norm_back(hat, inv, b.gainm[...], djn)
    b.gg_0[:, narrow : 5 * narrow] = gradm
    b.gg_0[:, 5 * narrow :] = grad3
    b.dsec[...] = jnp.concatenate(
        [djoined[:, k * narrow : (k + 1) * narrow] for k in range(4)], axis=0
    )
    put_pieces(b.idx5, b.dsec[...], b.row5, b.col5)
    flying = exchange(5)
    store_parts(b.gm, dot_tn(b.mnorm[...], dmerged), 0)
    redm.first_away()
    redm.first_own()
    red3.second()
    pick = Pick(ways[5].index(b.win2[...], t0, t1, as_quad, quads), b.dsec[...], halos[5])
    early = early_windows(rows, cols, NEAR)
    halves = [range(early), range(early, n2 // SLOT)]
    for half in halves:
        part = slice(half.start * SLOT, half.stop * SLOT)
        if half.start == 0:
            b.dsec2[part] = pick.part[part].astype(BF16)
        else:
            b.dsec2[part] = pick.finish(flying, part)
        dmixed = dot_nt(b.dsec2[part], b.proj2[...]).astype(BF16)
        for w in half:
            at = slice(w * SLOT, (w + 1) * SLOT)
            here = slice(at.start - part.start, at.stop - part.start)
            for g in range(narrow // LANES):
                lanes = lanes_of(narrow, g)
                qs = stack_heads(b.packed[at, lanes[0]], masks)
                k, v = b.packed[at, lanes[1]], b.packed[at, lanes[2]]
                weights = b.kept[w * (narrow // LANES) + g]
                back = unit_back(
                    qs, k, v, weights, weights.astype(BF16), dmixed[here, lanes[0]], masks
                )
                for t in range(3):
                    b.dpacked[at, lanes[t]] = back[t]
            if w == 0:
                redm.second()
            if w in (1, 2, 3):
                red3.third(1)
    drolled = dot_nt(b.dpacked[...], b.qkv2[...]).astype(BF16)
    hat, inv = norm_parts(b.tok2[...].astype(F32))
    dtok2, grad2 = norm_back(hat, inv, b.gain2[...], drolled.astype(F32))
    dtok2 = b.dsec2[...] + dtok2
    put_pieces(b.idx6, dtok2, b.row6, b.col6)
    flying = exchange(6)
    b.gg_0[:, :narrow] = grad2
    redg.first()
    store_parts(b.g2, dot_tn(b.rolled[...], b.dpacked[...]), 0)
    store_parts(b.g2, dot_tn(b.mixed[...], b.dsec2[...]), 3 * narrow)
    redg.second()
    red2.first_away()
    red2.first_own()
    red3.third()
    total = pick_o.finish(flying_o)
    for r in range(rows3):
        b.out[r] = total[r * pitch3 : r * pitch3 + cols3]
    pick = Pick(ways[6].index(b.nat[...], s0, s1, as_win, n2), dtok2, halos[6])
    red2.second()
    redm.third()
    total = pick.finish(flying)
    for r in range(rows):
        b.dtok[r] = total[r * pitch : r * pitch + cols]
    redg.third()
    red2.third()
    b.sum3[...] = red3.finish().astype(BF16)
    b.summ[...] = redm.finish().astype(BF16)
    b.sum2[...] = red2.finish().astype(BF16)
    b.gains[...] = redg.finish()


def finish_kernel(out, dtok, gains, sum3, summ, sum2, o_out, o_dtok, o_gains, *rest):
    o_out[...] = out[...]
    o_dtok[...] = dtok[...]
    for j in range(o_gains.shape[0]):
        o_gains[j : j + 1, :] = gains[:, j * LANES : (j + 1) * LANES]
    flats, rooms = rest[: len(rest) // 2], rest[len(rest) // 2 :]
    wide, narrow = sum3.shape[1] // 4, sum2.shape[1] // 4
    views = (
        (sum2, 0, 3 * narrow), (sum2, 3 * narrow, narrow), (summ, 0, wide),
        (sum3, 0, 3 * wide), (sum3, 3 * wide, wide),
    )
    for (source, offset, width), flat, room in zip(views, flats, rooms, strict=True):
        steps = width // LANES
        for j in range(steps):
            piece = source[:, offset + j * LANES : offset + (j + 1) * LANES]
            room[pl.ds(j, source.shape[0], stride=steps), :] = piece.astype(F32)
        flat[...] = room[...].astype(BF16)


def on_device(
    tokens, cotangent, shifts, norm2_gain, qkv2, proj2, merge_gain, merge_weight, norm3_gain,
    qkv3, proj3,
):
    rows, cols, narrow = tokens.shape
    wide = qkv3.shape[0]
    rows3, cols3 = rows // 2, cols // 2
    pitch, pitch3 = pitch_of(cols), pitch_of(cols3)
    base, base3 = padded(rows * cols), rows3 * pitch3
    win2, win3 = window_tokens(rows, cols), window_tokens(rows3, cols3)
    n2, n3 = len(win2[0]), len(win3[0])
    quad = quad_tokens(rows, cols)
    nat = grid_tokens(rows, cols, pitch)
    grid3 = grid_tokens(rows3, cols3, pitch3)
    as_quad = lambda h, w: quad_index(h, w, rows, cols)
    as_win = lambda h, w: win_index(h, w, cols)
    as_win3 = lambda h, w: win_index(h, w, cols3)
    ways = shifts_of(rows, cols, rows3, cols3)
    gain2, gainm, gain3 = (g.reshape(1, -1) for g in (norm2_gain, merge_gain, norm3_gain))
    nr, nc = lax.axis_size("rows"), lax.axis_size("cols")
    chips = nc // 2
    quads, gains = len(quad[0]), 5 * narrow + wide
    codes = dict(
        win2=coded(win2), win3=coded(win3), quad=coded(quad), nat=coded(nat), grid3=coded(grid3),
        idx2=ways[2].pieces(as_win), idx4=ways[4].pieces(as_win3), idx5=ways[5].pieces(as_quad),
        idx6=ways[6].pieces(as_win), idx7=ways[7].pieces(as_win3),
    )
    inputs = dict(
        tok=tokens, cot=cotangent, shifts=shifts, codes=np.concatenate(list(codes.values())),
        rwin2=coded(win2)[:, 0].reshape(-1, SLOT), rwin3=coded(win3)[:, 0].reshape(-1, SLOT),
        gain2=gain2, gainm=gainm, gain3=gain3, qkv2=qkv2, proj2=proj2,
        weight=merge_weight, qkv3=qkv3, proj3=proj3,
    )
    m3, mm, m2 = wide // (nr * nc), 4 * narrow // (nr * nc), narrow // (nr * nc)
    outs = dict(
        out=(cotangent.shape, BF16),
        dtok=(tokens.shape, BF16),
        gains=((1, gains), F32),
        sum3=((m3, 4 * wide), BF16),
        summ=((mm, wide), BF16),
        sum2=((m2, 4 * narrow), BF16),
    )
    scratch = dict(
        toks=((base, narrow), BF16), cots=((base3, wide), BF16),
        tok2=((n2, narrow), BF16),
        rolled=((n2, narrow), BF16), packed=((n2, 3 * narrow), BF16), mixed=((n2, narrow), BF16),
        joined=((base3, 4 * narrow), BF16), mnorm=((base3, 4 * narrow), BF16),
        merged=((base3, wide), BF16), merged3=((n3, wide), BF16), rolled3=((n3, wide), BF16),
        dproj3=((n3, wide), BF16),
        packed3=((n3, 3 * wide), BF16), mixed3=((n3, wide), BF16),
        dpacked3=((n3, 3 * wide), BF16), dsec=((quads, narrow), BF16),
        dsec2=((n2, narrow), BF16), dpacked=((n2, 3 * narrow), BF16),
    )
    kept = (n2 // SLOT * (narrow // LANES), PACK * SLOT, SLOT)
    ints = dict(lc2=(n2, SLOT), lr2=(n2 // SLOT, SLOT), lc3=(n3, SLOT), lr3=(n3 // SLOT, SLOT))
    scratch |= {name: (shape, jnp.int32) for name, shape in ints.items()}
    scratch["kept"] = (kept, F32)
    for name in LATE:
        scratch["v_" + name] = (inputs[name].shape, inputs[name].dtype)
    copies = len(ways) * 3
    for n, way in enumerate(ways):
        width = narrow if way.rows == rows else wide
        if n not in (0, 1, 3):
            scratch[f"row{n}"] = ((way.row, width), BF16)
        scratch[f"col{n}"] = ((way.col, width), BF16)
        for i, size in enumerate(way.sizes()):
            scratch[f"h{n}_{i}"] = ((size, width), BF16)
    for name, shape in (("g3", (m3, 4 * wide)), ("gm", (mm, wide)), ("g2", (m2, 4 * narrow))):
        scratch[name] = ((2, chips, nr) + shape, BF16)
        for i, lead in enumerate(
            ((chips, nr), (chips, nr), (max(chips - 1, 1), nr), (nr,), (max(nr - 1, 1),))
        ):
            scratch[f"{name}_{i}"] = (lead + shape, BF16)
        copies += chips + (chips - 1) * nr + nr - 1
    for i, lead in enumerate(((), (), (), (max(chips - 1, 1),), (), (max(nr - 1, 1),))):
        scratch[f"gg_{i}"] = (lead + (1, gains), F32)
    copies += chips + nr - 1
    spaces = [pltpu.VMEM(s, d) for s, d in scratch.values()]
    spaces += [pltpu.SemaphoreType.DMA((n,)) for n in (copies, copies, len(LATE))]
    results = pl.pallas_call(
        functools.partial(
            whole_kernel, {k: len(v) for k, v in codes.items()}, list(inputs), list(outs), list(scratch) + ["send", "recv", "loaded"]
        ),
        out_shape=[jax.ShapeDtypeStruct(s, d) for s, d in outs.values()],
        in_specs=[
            pl.BlockSpec(
                memory_space=pltpu.SMEM if name == "shifts" else pl.ANY if name in LATE else pltpu.VMEM
            )
            for name in inputs
        ],
        out_specs=[pl.BlockSpec(memory_space=pltpu.VMEM)] * len(outs),
        scratch_shapes=spaces,
        compiler_params=pltpu.CompilerParams(
            collective_id=0, has_side_effects=True, vmem_limit_bytes=60 * 2**20
        ),
        name="block",
    )(*inputs.values())
    flats = [
        (m * width // LANES, LANES)
        for m, width in (
            (m2, 3 * narrow), (m2, narrow), (mm, wide), (m3, 3 * wide), (m3, wide)
        )
    ]
    final = pl.pallas_call(
        finish_kernel,
        out_shape=[
            jax.ShapeDtypeStruct(cotangent.shape, BF16),
            jax.ShapeDtypeStruct(tokens.shape, BF16),
            jax.ShapeDtypeStruct((gains // LANES, LANES), F32),
        ]
        + [jax.ShapeDtypeStruct(shape, BF16) for shape in flats],
        scratch_shapes=[pltpu.VMEM(shape, F32) for shape in flats],
        name="finish",
    )(*results)
    return tuple(final[:2]) + tuple(x.reshape(-1) for x in final[2:])


def solution(mesh):
    tile = P(("groups", "rows"), "cols", None)
    spread = P(("groups", "rows", "cols"))
    return jax.shard_map(
        on_device,
        mesh=mesh,
        in_specs=(tile, tile) + (P(),) * 9,
        out_specs=(tile, tile, P("groups")) + (spread,) * 5,
        check_vma=False,
    )
```

```python
import functools

import jax
import jax.numpy as jnp
import numpy as np
from jax import lax
from jax.experimental import pallas as pl
from jax.experimental.pallas import tpu as pltpu
from jax.sharding import PartitionSpec as P

HEAD = 32
WIN = 7
MARGIN = WIN - 1
NEAR = 4
SLOT = 64
LANES = 128
EPSILON = 1e-05
MASKED = -100.0
F32 = jnp.float32
BF16 = jnp.bfloat16


def pitch_of(count):
    return -(-count // 16) * 16


def window_tokens(rows, cols):
    h, w, ok = [], [], []
    for wr in range(rows // WIN):
        for wc in range(cols // WIN):
            for t in range(SLOT):
                good = t < WIN * WIN
                h.append(wr * WIN + t // WIN if good else 0)
                w.append(wc * WIN + t % WIN if good else 0)
                ok.append(good)
    return np.array(h, np.int32), np.array(w, np.int32), np.array(ok)


def grid_tokens(rows, cols, pitch):
    h = np.repeat(np.arange(rows, dtype=np.int32), pitch)
    w = np.tile(np.arange(pitch, dtype=np.int32), rows)
    ok = w < cols
    return h, np.where(ok, w, 0).astype(np.int32), ok


def quad_tokens(rows, cols):
    a, b, ok = grid_tokens(rows // 2, cols // 2, pitch_of(cols // 2))
    h = np.concatenate([2 * a + (k & 1) for k in range(4)])
    w = np.concatenate([2 * b + (k >> 1) for k in range(4)])
    return h, w, np.tile(ok, 4)


def by_window(x):
    return (x * 9363) >> 16


def win_index(h, w, cols):
    hq, wq = by_window(h), by_window(w)
    return (hq * (cols // WIN) + wq) * SLOT + (h - hq * WIN) * WIN + w - wq * WIN


def quad_index(h, w, rows, cols):
    pitch = pitch_of(cols // 2)
    return ((h & 1) + 2 * (w & 1)) * ((rows // 2) * pitch) + (h >> 1) * pitch + (w >> 1)


def spread(values):
    return np.repeat(values.astype(np.int32).reshape(-1, 1), LANES, axis=1)


def coded(tokens):
    h, w, ok = tokens
    return spread(np.where(ok, h * 4096 + w, -1))


def decoded(code):
    return code >> 12, code & 4095, code >= 0


def padded(count):
    return -(-count // 16) * 16


class Shift:
    def __init__(self, rows, cols, margin, behind, pitch=None):
        self.rows, self.cols, self.margin, self.behind = rows, cols, margin, behind
        self.pitch = pitch or cols
        self.row = padded(margin * self.pitch)
        self.col = padded(rows * margin)
        self.first = (rows - margin) * margin // 16 * 16 if behind else 0
        self.corner = (self.col if behind else padded(margin * margin)) - self.first
        self.by = 1 if behind else -1
        self.extra = self.row + self.col + self.corner

    def sizes(self):
        return self.row, self.col, self.corner

    def index(self, code, by_rows, by_cols, inner, base):
        h, w, ok = decoded(code)
        m, rows, cols = self.margin, self.rows, self.cols
        if self.behind:
            h2, w2 = h - by_rows, w - by_cols
            local = inner(jnp.maximum(h2, 0), jnp.maximum(w2, 0))
            out_row, out_col = h2 < 0, w2 < 0
            r, c = h2 + m, w2 + m
            corner = (h2 + rows) * m - self.first + c
        else:
            h2, w2 = h + by_rows, w + by_cols
            local = inner(jnp.minimum(h2, rows - 1), jnp.minimum(w2, cols - 1))
            out_row, out_col = h2 >= rows, w2 >= cols
            r, c = h2 - rows, w2 - cols
            corner = r * m + c
        row = base + r * self.pitch + w2
        side = base + self.row + h2 * m + c
        corner = base + self.row + self.col + corner
        got = jnp.where(
            out_row, jnp.where(out_col, corner, row), jnp.where(out_col, side, local)
        )
        return jnp.where(ok, got, -1)

    def pieces(self, inner):
        m = self.margin
        top = self.rows - m if self.behind else 0
        left = self.cols - m if self.behind else 0
        parts = []
        for count, wide, pitch, h0, w0, size in (
            (m, self.cols, self.pitch, top, 0, self.row),
            (self.rows, m, m, 0, left, self.col),
        ):
            h, w, ok = grid_tokens(count, wide, pitch)
            got = np.where(ok, inner(h + h0, w + w0), -1)
            parts.append(np.pad(got, (0, size - len(got)), constant_values=-1))
        return spread(np.concatenate(parts))


def window_labels(code, rows, cols, axis_row, axis_col, shift_rows, shift_cols):
    h, w, ok = decoded(code)
    height = rows * lax.axis_size("rows")
    breadth = cols * lax.axis_size("cols")
    gh = axis_row * rows + h
    gw = axis_col * cols + w
    lh = jnp.where(gh < height - WIN, 0, jnp.where(gh < height - shift_rows, 1, 2))
    lw = jnp.where(gw < breadth - WIN, 0, jnp.where(gw < breadth - shift_cols, 1, 2))
    return jnp.where(ok, lh * 3 + lw, -1)


def dot(a, b):
    return jnp.dot(a, b, preferred_element_type=F32)


def dot_nt(a, b):
    return lax.dot_general(a, b, (((1,), (1,)), ((), ())), preferred_element_type=F32)


def dot_tn(a, b):
    return lax.dot_general(a, b, (((0,), (0,)), ((), ())), preferred_element_type=F32)


def one_hot(idx, count):
    lane = lax.broadcasted_iota(jnp.int32, (1, LANES), 1)
    parts = []
    for start in range(0, count, LANES):
        wide = min(LANES, count - start)
        parts.append(jnp.where(idx[:, :wide] == lane[:, :wide] + start, 1.0, 0.0).astype(BF16))
    return jnp.concatenate(parts, axis=1)


def picked(hot, source):
    return dot(hot, source).astype(BF16)


def select(idx, source):
    return picked(one_hot(idx, source.shape[0]), source)


def norm_parts(x):
    centred = x - jnp.mean(x, axis=-1, keepdims=True)
    inverse = lax.rsqrt(jnp.mean(centred * centred, axis=-1, keepdims=True) + EPSILON)
    return centred * inverse, inverse


def norm_back(hat, inverse, gain, dy):
    grad_gain = jnp.sum(dy * hat, axis=0, keepdims=True)
    t = dy * gain
    dx = inverse * (
        t
        - jnp.mean(t, axis=-1, keepdims=True)
        - hat * jnp.mean(t * hat, axis=-1, keepdims=True)
    )
    return dx.astype(BF16), grad_gain


PACK = LANES // HEAD


def head_masks():
    lane = lax.broadcasted_iota(jnp.int32, (1, LANES), 1) // HEAD
    return [jnp.where(lane == h, 1.0, 0.0).astype(BF16) for h in range(PACK)]


def stack_heads(x, masks):
    return jnp.concatenate([x * m for m in masks], axis=0)


def pick_heads(o):
    lane = lax.broadcasted_iota(jnp.int32, (SLOT, LANES), 1) // HEAD
    out = o[:SLOT]
    for h in range(1, PACK):
        out = jnp.where(lane == h, o[h * SLOT : (h + 1) * SLOT], out)
    return out


def window_bias(lc_ref, lr_ref, w):
    lc = lc_ref[w * SLOT : (w + 1) * SLOT, :]
    lr = lr_ref[w : w + 1, :]
    bias = jnp.where((lc == lr) | (lc < 0), 0.0, MASKED)
    bias = jnp.where(lr < 0, -1e30, bias)
    return jnp.concatenate([bias] * PACK, axis=0)


def soft(qs, k, bias):
    raised = jnp.exp(dot_nt(qs, k) * HEAD ** (-0.5) + bias)
    return raised * (1.0 / jnp.sum(raised, axis=-1, keepdims=True))


def unit_back(qs, k, v, weights, wb, dm, masks):
    dms = stack_heads(dm, masks)
    dw = dot_nt(dms, v).astype(BF16).astype(F32)
    ds = weights * (dw - jnp.sum(dw * weights, axis=-1, keepdims=True))
    ds = (ds * HEAD ** (-0.5)).astype(BF16)
    dq = pick_heads(dot(ds, k))
    dk = dot_tn(ds, qs)
    dv = dot_tn(wb, dms)
    return dq.astype(BF16), dk.astype(BF16), dv.astype(BF16)


def fill_tile(scratch, tile, pitch):
    count, wide, _ = tile.shape
    for r in range(count):
        scratch[r * pitch : r * pitch + wide, :] = tile[r]


LATE = ("qkv2", "proj2", "weight", "proj3", "qkv3", )


class Load:
    def __init__(self, copy):
        self.copy, self.flying = copy, True
        copy.start()

    def wait(self):
        if self.flying:
            self.copy.wait()
        self.flying = False


class Bag:
    pass


MESH = pl.DeviceIdType.MESH


class Links:
    def __init__(self, send, recv):
        self.send, self.recv, self.used = send, recv, 0
        self.group = lax.axis_index("groups")
        self.row, self.col = lax.axis_index("rows"), lax.axis_index("cols")
        self.nr, self.nc = lax.axis_size("rows"), lax.axis_size("cols")
        self.core, self.chip = lax.rem(self.col, 2), self.col // 2
        self.chips = self.nc // 2

    def device(self, dr, dc):
        row = lax.rem(self.row + dr + self.nr, self.nr)
        col = lax.rem(self.col + dc + self.nc, self.nc)
        return (self.group, row, col)

    def partner(self):
        return (self.group, self.row, self.chip * 2 + 1 - self.core)

    def greet(self):
        offsets = {(d, 0) for d in range(1, self.nr)} | {(0, d) for d in range(1, self.nc)}
        offsets |= {(1, 1), (self.nr - 1, self.nc - 1)}
        self.greeted = len(offsets)
        sem = pltpu.get_barrier_semaphore()
        for dr, dc in sorted(offsets):
            pl.semaphore_signal(sem, inc=1, device_id=self.device(dr, dc), device_id_type=MESH)

    def barrier(self):
        pl.semaphore_wait(pltpu.get_barrier_semaphore(), self.greeted)

    def start(self, source, target, device):
        copy = pltpu.make_async_remote_copy(
            src_ref=source,
            dst_ref=target,
            send_sem=self.send.at[self.used],
            recv_sem=self.recv.at[self.used],
            device_id=device,
            device_id_type=MESH,
        )
        self.used += 1
        copy.start()
        return copy

    def exchange(self, shift, row, col, halo):
        by = shift.by
        corner = col.at[shift.first : shift.first + shift.corner]
        return [
            self.start(corner, halo[2], self.device(by, by)),
            self.start(row, halo[0], self.device(by, 0)),
            self.start(col, halo[1], self.device(0, by)),
        ]


def wait_all(copies):
    for copy in copies:
        copy.wait()


class Reduction:
    def __init__(self, links, kind, parts, bufs, whole=False):
        self.links, self.kind, self.parts, self.whole = links, kind, parts, whole
        self.got1, self.half, self.got2, self.part, self.got3 = bufs
        self.arriving, self.sent, self.copies, self.step = {}, 1, [], 1


    def start_first(self, d):
        k = self.links
        x = lax.rem(k.chip + d, k.chips)
        return k.start(self.parts.at[1 - k.core, x], self.got1.at[x], k.partner())

    def first_away(self):
        k = self.links
        if self.whole:
            self.own = k.start(self.parts.at[1 - k.core], self.got1, k.partner())
            self.away = [self.own]
        else:
            self.away = [self.start_first(d) for d in range(1, k.chips)]

    def first_own(self):
        if not self.whole:
            self.own = self.start_first(0)

    def both_cores(self, x, r):
        return self.parts[self.links.core, x, r].astype(F32) + self.got1[x, r].astype(F32)

    def second(self, steps=99):
        k = self.links
        if self.whole:
            wait_all(self.away)
            for d in range(1, k.chips):
                x = lax.rem(k.chip + d, k.chips)
                for r in range(k.nr):
                    self.half[x, r] = self.both_cores(x, r).astype(self.kind)
                self.arriving[1, d] = k.start(
                    self.half.at[x], self.got2.at[d - 1], k.device(0, 2 * d)
                )
            return
        if not self.arriving:
            wait_all(self.away)
        for e in range(self.sent, min(self.sent + steps, k.nr + 1)):
            r = lax.rem(k.row + e, k.nr)
            for d in range(1, k.chips):
                x = lax.rem(k.chip + d, k.chips)
                self.half[x, r] = self.both_cores(x, r).astype(self.kind)
                self.arriving[e, d] = k.start(
                    self.half.at[x, r], self.got2.at[d - 1, r], k.device(0, 2 * d)
                )
        self.sent += steps

    def third(self, steps=None):
        k = self.links
        if self.step == 1 and not self.whole:
            self.own.wait()
        stop = k.nr + 1 if steps is None else min(self.step + steps, k.nr + 1)
        for e in range(self.step, stop):
            r = lax.rem(k.row + e, k.nr)
            total = self.both_cores(k.chip, r)
            for d in range(1, k.chips):
                if (e, d) in self.arriving:
                    self.arriving[e, d].wait()
                total = total + self.got2[d - 1, r].astype(F32)
            self.part[r] = total.astype(self.kind)
            if e < k.nr:
                self.copies.append(k.start(self.part.at[r], self.got3.at[e - 1], k.device(e, 0)))
        self.step = stop

    def finish(self):
        k = self.links
        wait_all(self.copies)
        total = self.part[k.row].astype(F32)
        for d in range(1, k.nr):
            total = total + self.got3[d - 1].astype(F32)
        return total


class GainSum:
    def __init__(self, links, bufs):
        self.links = links
        self.own, self.got1, self.half, self.got2, self.part, self.got3 = bufs

    def first(self):
        self.copies = [self.links.start(self.own, self.got1, self.links.partner())]

    def second(self):
        k = self.links
        wait_all(self.copies)
        self.half[...] = self.own[...] + self.got1[...]
        self.copies = [
            k.start(self.half, self.got2.at[d - 1], k.device(0, 2 * d)) for d in range(1, k.chips)
        ]

    def third(self):
        k = self.links
        wait_all(self.copies)
        total = self.half[...]
        for d in range(1, k.chips):
            total = total + self.got2[d - 1]
        self.part[...] = total
        self.copies = [k.start(self.part, self.got3.at[d - 1], k.device(d, 0)) for d in range(1, k.nr)]

    def finish(self):
        wait_all(self.copies)
        total = self.part[...]
        for d in range(1, self.links.nr):
            total = total + self.got3[d - 1]
        return total


def store_parts(parts, value, offset):
    _, chips, nr, depth, _ = parts.shape
    width = value.shape[1]
    for r in range(nr):
        for x in range(chips):
            for core in range(2):
                i = (r * chips + x) * 2 + core
                piece = value[i * depth : (i + 1) * depth]
                parts[core, x, r, :, offset : offset + width] = piece.astype(BF16)


def fill_side(scratch, tile, margin):
    scratch[...] = jnp.zeros_like(scratch)
    for r in range(tile.shape[0]):
        scratch[r * margin : (r + 1) * margin, :] = tile[r, :margin, :]


def put_pieces(idx, source, row_ref, col_ref):
    got = select(idx[...], source)
    row_ref[...] = got[: row_ref.shape[0]]
    col_ref[...] = got[row_ref.shape[0] :]


def lanes_of(width, g):
    return [slice(t * width + g * LANES, t * width + (g + 1) * LANES) for t in range(3)]


def shifts_of(rows, cols, rows3, cols3):
    pitch3 = pitch_of(cols3)
    return (
        Shift(rows, cols, MARGIN, False),
        Shift(rows3, cols3, MARGIN, False, pitch3),
        Shift(rows, cols, NEAR, True),
        Shift(rows3, cols3, MARGIN, False, pitch3),
        Shift(rows3, cols3, MARGIN, True),
        Shift(rows, cols, NEAR, False),
        Shift(rows, cols, MARGIN, True),
        Shift(rows3, cols3, MARGIN, True),
    )


class Pick:
    def __init__(self, idx, local, halo):
        base, extra = local.shape[0], sum(h.shape[0] for h in halo)
        self.part = dot(one_hot(idx, base), local)
        self.hot = one_hot(idx - base, extra)
        self.halo = halo

    def finish(self, flying, at=slice(None)):
        wait_all(flying)
        rest = jnp.concatenate([h[...] for h in self.halo], axis=0)
        return (self.part[at] + dot(self.hot[at], rest)).astype(BF16)


def early_windows(rows, cols, margin):
    if 2 * WIN + margin > rows + WIN:
        return 0
    return (cols - margin) // WIN


def whole_kernel(code_sizes, in_names, out_names, scratch_names, *refs):
    b = Bag()
    for name, ref in zip(in_names + out_names + scratch_names, refs, strict=True):
        setattr(b, name, ref)
    links = Links(b.send, b.recv)
    links.greet()
    at = 0
    for name, size in code_sizes.items():
        setattr(b, name, b.codes.at[at : at + size])
        at += size
    loads = {}
    for n, name in enumerate(LATE):
        kept = getattr(b, "v_" + name)
        loads[name] = Load(pltpu.make_async_copy(getattr(b, name), kept, b.loaded.at[n]))
        setattr(b, name, kept)
    rows, cols, narrow = b.tok.shape
    rows3, cols3, wide = b.cot.shape
    pitch, pitch3 = pitch_of(cols), pitch_of(cols3)
    red3 = Reduction(links, BF16, b.g3, [getattr(b, f"g3_{i}") for i in range(5)])
    redm = Reduction(links, BF16, b.gm, [getattr(b, f"gm_{i}") for i in range(5)], True)
    red2 = Reduction(links, BF16, b.g2, [getattr(b, f"g2_{i}") for i in range(5)], True)
    redg = GainSum(links, [getattr(b, f"gg_{i}") for i in range(6)])
    ways = shifts_of(rows, cols, rows3, cols3)
    halos = [[getattr(b, f"h{n}_{i}") for i in range(3)] for n in range(len(ways))]
    row_of = [getattr(b, f"row{n}") if hasattr(b, f"row{n}") else None for n in range(len(ways))]
    col_of = [getattr(b, f"col{n}") for n in range(len(ways))]
    masks = head_masks()
    s0, s1, s2, s3 = (b.shifts[i] for i in range(4))
    e0 = jnp.minimum(s0 - (s0 & 1), 2 * s2)
    e1 = jnp.minimum(s1 - (s1 & 1), 2 * s3)
    t0, t1 = s0 - e0, s1 - e1
    d0, d1 = s2 - (e0 >> 1), s3 - (e1 >> 1)
    quads, n2, n3 = b.quad.shape[0], b.win2.shape[0], b.win3.shape[0]
    base, base3 = b.toks.shape[0], rows3 * pitch3
    as_toks = lambda h, w: h * cols + w
    as_grid3 = lambda h, w: h * pitch3 + w
    as_quad = lambda h, w: quad_index(h, w, rows, cols)
    as_win = lambda h, w: win_index(h, w, cols)
    as_win3 = lambda h, w: win_index(h, w, cols3)

    def exchange(n, row=None):
        row = row_of[n] if row is None else row
        return links.exchange(ways[n], row, col_of[n], halos[n])

    if base > rows * cols:
        b.toks[rows * cols :, :] = jnp.zeros((base - rows * cols, narrow), BF16)
    fill_tile(b.toks, b.tok, cols)
    fill_side(b.col0, b.tok, MARGIN)
    b.cots[...] = jnp.zeros_like(b.cots)
    fill_tile(b.cots, b.cot, pitch3)
    fill_side(b.col1, b.cot, MARGIN)
    links.barrier()
    flying = exchange(0, b.toks.at[0 : ways[0].row])
    flying_c = exchange(1, b.cots.at[0 : ways[1].row])

    pick = Pick(ways[0].index(b.win2[...], s0, s1, as_toks, base), b.toks[...], halos[0])
    place2 = (rows, cols, links.row, links.col, s0, s1)
    place3 = (rows3, cols3, links.row, links.col, s2, s3)
    b.lc2[...] = window_labels(b.win2[:, :SLOT], *place2)
    b.lr2[...] = window_labels(b.rwin2[...], *place2)
    b.lc3[...] = window_labels(b.win3[:, :SLOT], *place3)
    b.lr3[...] = window_labels(b.rwin3[...], *place3)
    early = early_windows(rows, cols, MARGIN)
    for half in (range(early), range(early, n2 // SLOT)):
        part = slice(half.start * SLOT, half.stop * SLOT)
        tok2 = pick.finish(flying, part) if half.start else pick.part[part].astype(BF16)
        b.tok2[part] = tok2
        hat, _ = norm_parts(tok2.astype(F32))
        b.rolled[part] = (hat * b.gain2[...]).astype(BF16)
        if half.start == 0:
            loads["qkv2"].wait()
        b.packed[part] = dot(b.rolled[part], b.qkv2[...]).astype(BF16)
        for w in half:
            bias = window_bias(b.lc2, b.lr2, w)
            at = slice(w * SLOT, (w + 1) * SLOT)
            for g in range(narrow // LANES):
                lanes = lanes_of(narrow, g)
                qs = stack_heads(b.packed[at, lanes[0]], masks)
                weights = soft(qs, b.packed[at, lanes[1]], bias)
                b.kept[w * (narrow // LANES) + g] = weights
                wb = weights.astype(BF16)
                b.mixed[at, lanes[0]] = pick_heads(dot(wb, b.packed[at, lanes[2]])).astype(BF16)
    loads["proj2"].wait()
    win = dot(b.mixed[...], b.proj2[...]).astype(BF16)
    section = (b.tok2[...].astype(F32) + win.astype(F32)).astype(BF16)
    put_pieces(b.idx2, section, b.row2, b.col2)
    flying = exchange(2)

    pick = Pick(ways[2].index(b.quad[...], t0, t1, as_win, n2), section, halos[2])
    pick_c = Pick(ways[1].index(b.win3[...], s2, s3, as_grid3, base3), b.cots[...], halos[1])
    section = pick.finish(flying)
    t3 = rows3 * pitch3
    joined = jnp.concatenate([section[k * t3 : (k + 1) * t3] for k in range(4)], axis=1)
    b.joined[...] = joined
    hat, _ = norm_parts(joined.astype(F32))
    b.mnorm[...] = (hat * b.gainm[...]).astype(BF16)
    loads["weight"].wait()
    merged = dot(b.mnorm[...], b.weight[...]).astype(BF16)
    b.merged[...] = merged
    b.col3[...] = jnp.zeros_like(b.col3)
    for r in range(rows3):
        b.col3[r * MARGIN : (r + 1) * MARGIN, :] = merged[r * pitch3 : r * pitch3 + MARGIN]
    flying = exchange(3, b.merged.at[0 : ways[3].row])

    pick = Pick(ways[3].index(b.win3[...], d0, d1, as_grid3, base3), merged, halos[3])
    b.dproj3[...] = pick_c.finish(flying_c)
    loads["proj3"].wait()
    dmixed = dot_nt(b.dproj3[...], b.proj3[...]).astype(BF16)
    merged3 = pick.finish(flying)
    b.merged3[...] = merged3
    hat, _ = norm_parts(merged3.astype(F32))
    rolled3 = (hat * b.gain3[...]).astype(BF16)
    b.rolled3[...] = rolled3
    loads["qkv3"].wait()
    b.packed3[...] = dot(rolled3, b.qkv3[...]).astype(BF16)
    for w in range(b.lr3.shape[0]):
        bias = window_bias(b.lc3, b.lr3, w)
        at = slice(w * SLOT, (w + 1) * SLOT)
        for g in range(wide // LANES):
            lanes = lanes_of(wide, g)
            qs = stack_heads(b.packed3[at, lanes[0]], masks)
            k, v = b.packed3[at, lanes[1]], b.packed3[at, lanes[2]]
            weights = soft(qs, k, bias)
            wb = weights.astype(BF16)
            b.mixed3[at, lanes[0]] = pick_heads(dot(wb, v)).astype(BF16)
            back = unit_back(qs, k, v, weights, wb, dmixed[at, lanes[0]], masks)
            for t in range(3):
                b.dpacked3[at, lanes[t]] = back[t]
    drolled3 = dot_nt(b.dpacked3[...], b.qkv3[...]).astype(BF16)
    hat, inv = norm_parts(b.merged3[...].astype(F32))
    dmerged3, grad3 = norm_back(hat, inv, b.gain3[...], drolled3.astype(F32))
    dmerged3 = b.dproj3[...] + dmerged3
    put_pieces(b.idx4, dmerged3, b.row4, b.col4)
    flying = exchange(4)
    store_parts(b.g3, dot_tn(b.rolled3[...], b.dpacked3[...]), 0)
    store_parts(b.g3, dot_tn(b.mixed3[...], b.dproj3[...]), 3 * wide)
    red3.first_away()
    red3.first_own()
    proj = dot(b.mixed3[...], b.proj3[...]).astype(BF16)
    out3 = (b.merged3[...].astype(F32) + proj.astype(F32)).astype(BF16)
    put_pieces(b.idx7, out3, b.row7, b.col7)
    flying_o = exchange(7)
    pick_o = Pick(ways[7].index(b.grid3[...], s2, s3, as_win3, n3), out3, halos[7])
    pick = Pick(ways[4].index(b.grid3[...], d0, d1, as_win3, n3), dmerged3, halos[4])
    red3.second(1)
    hat, inv = norm_parts(b.joined[...].astype(F32))
    dmerged = pick.finish(flying)
    djn = dot_nt(dmerged, b.weight[...]).astype(BF16).astype(F32)
    djoined, gradm = norm_back(hat, inv, b.gainm[...], djn)
    b.gg_0[:, narrow : 5 * narrow] = gradm
    b.gg_0[:, 5 * narrow :] = grad3
    b.dsec[...] = jnp.concatenate(
        [djoined[:, k * narrow : (k + 1) * narrow] for k in range(4)], axis=0
    )
    put_pieces(b.idx5, b.dsec[...], b.row5, b.col5)
    flying = exchange(5)
    store_parts(b.gm, dot_tn(b.mnorm[...], dmerged), 0)
    redm.first_away()
    redm.first_own()
    red3.second()
    pick = Pick(ways[5].index(b.win2[...], t0, t1, as_quad, quads), b.dsec[...], halos[5])
    early = early_windows(rows, cols, NEAR)
    halves = [range(early), range(early, n2 // SLOT)]
    for half in halves:
        part = slice(half.start * SLOT, half.stop * SLOT)
        if half.start == 0:
            b.dsec2[part] = pick.part[part].astype(BF16)
        else:
            b.dsec2[part] = pick.finish(flying, part)
        dmixed = dot_nt(b.dsec2[part], b.proj2[...]).astype(BF16)
        for w in half:
            at = slice(w * SLOT, (w + 1) * SLOT)
            here = slice(at.start - part.start, at.stop - part.start)
            for g in range(narrow // LANES):
                lanes = lanes_of(narrow, g)
                qs = stack_heads(b.packed[at, lanes[0]], masks)
                k, v = b.packed[at, lanes[1]], b.packed[at, lanes[2]]
                weights = b.kept[w * (narrow // LANES) + g]
                back = unit_back(
                    qs, k, v, weights, weights.astype(BF16), dmixed[here, lanes[0]], masks
                )
                for t in range(3):
                    b.dpacked[at, lanes[t]] = back[t]
            if w == 0:
                redm.second()
            if w in (0, 2, 3):
                red3.third(1)
    drolled = dot_nt(b.dpacked[...], b.qkv2[...]).astype(BF16)
    hat, inv = norm_parts(b.tok2[...].astype(F32))
    dtok2, grad2 = norm_back(hat, inv, b.gain2[...], drolled.astype(F32))
    dtok2 = b.dsec2[...] + dtok2
    put_pieces(b.idx6, dtok2, b.row6, b.col6)
    flying = exchange(6)
    b.gg_0[:, :narrow] = grad2
    redg.first()
    store_parts(b.g2, dot_tn(b.rolled[...], b.dpacked[...]), 0)
    store_parts(b.g2, dot_tn(b.mixed[...], b.dsec2[...]), 3 * narrow)
    redg.second()
    red2.first_away()
    red2.first_own()
    red3.third()
    total = pick_o.finish(flying_o)
    for r in range(rows3):
        b.out[r] = total[r * pitch3 : r * pitch3 + cols3]
    pick = Pick(ways[6].index(b.nat[...], s0, s1, as_win, n2), dtok2, halos[6])
    red2.second()
    redm.third()
    total = pick.finish(flying)
    for r in range(rows):
        b.dtok[r] = total[r * pitch : r * pitch + cols]
    redg.third()
    red2.third()
    b.sum3[...] = red3.finish().astype(BF16)
    b.summ[...] = redm.finish().astype(BF16)
    b.sum2[...] = red2.finish().astype(BF16)
    b.gains[...] = redg.finish()


def finish_kernel(out, dtok, gains, sum3, summ, sum2, o_out, o_dtok, o_gains, *rest):
    o_out[...] = out[...]
    o_dtok[...] = dtok[...]
    for j in range(o_gains.shape[0]):
        o_gains[j : j + 1, :] = gains[:, j * LANES : (j + 1) * LANES]
    flats, rooms = rest[: len(rest) // 2], rest[len(rest) // 2 :]
    wide, narrow = sum3.shape[1] // 4, sum2.shape[1] // 4
    views = (
        (sum2, 0, 3 * narrow), (sum2, 3 * narrow, narrow), (summ, 0, wide),
        (sum3, 0, 3 * wide), (sum3, 3 * wide, wide),
    )
    for (source, offset, width), flat, room in zip(views, flats, rooms, strict=True):
        steps = width // LANES
        for j in range(steps):
            piece = source[:, offset + j * LANES : offset + (j + 1) * LANES]
            room[pl.ds(j, source.shape[0], stride=steps), :] = piece.astype(F32)
        flat[...] = room[...].astype(BF16)


def on_device(
    tokens, cotangent, shifts, norm2_gain, qkv2, proj2, merge_gain, merge_weight, norm3_gain,
    qkv3, proj3,
):
    rows, cols, narrow = tokens.shape
    wide = qkv3.shape[0]
    rows3, cols3 = rows // 2, cols // 2
    pitch, pitch3 = pitch_of(cols), pitch_of(cols3)
    base, base3 = padded(rows * cols), rows3 * pitch3
    win2, win3 = window_tokens(rows, cols), window_tokens(rows3, cols3)
    n2, n3 = len(win2[0]), len(win3[0])
    quad = quad_tokens(rows, cols)
    nat = grid_tokens(rows, cols, pitch)
    grid3 = grid_tokens(rows3, cols3, pitch3)
    as_quad = lambda h, w: quad_index(h, w, rows, cols)
    as_win = lambda h, w: win_index(h, w, cols)
    as_win3 = lambda h, w: win_index(h, w, cols3)
    ways = shifts_of(rows, cols, rows3, cols3)
    gain2, gainm, gain3 = (g.reshape(1, -1) for g in (norm2_gain, merge_gain, norm3_gain))
    nr, nc = lax.axis_size("rows"), lax.axis_size("cols")
    chips = nc // 2
    quads, gains = len(quad[0]), 5 * narrow + wide
    codes = dict(
        win2=coded(win2), win3=coded(win3), quad=coded(quad), nat=coded(nat), grid3=coded(grid3),
        idx2=ways[2].pieces(as_win), idx4=ways[4].pieces(as_win3), idx5=ways[5].pieces(as_quad),
        idx6=ways[6].pieces(as_win), idx7=ways[7].pieces(as_win3),
    )
    inputs = dict(
        tok=tokens, cot=cotangent, shifts=shifts, codes=np.concatenate(list(codes.values())),
        rwin2=coded(win2)[:, 0].reshape(-1, SLOT), rwin3=coded(win3)[:, 0].reshape(-1, SLOT),
        gain2=gain2, gainm=gainm, gain3=gain3, qkv2=qkv2, proj2=proj2,
        weight=merge_weight, qkv3=qkv3, proj3=proj3,
    )
    m3, mm, m2 = wide // (nr * nc), 4 * narrow // (nr * nc), narrow // (nr * nc)
    outs = dict(
        out=(cotangent.shape, BF16),
        dtok=(tokens.shape, BF16),
        gains=((1, gains), F32),
        sum3=((m3, 4 * wide), BF16),
        summ=((mm, wide), BF16),
        sum2=((m2, 4 * narrow), BF16),
    )
    scratch = dict(
        toks=((base, narrow), BF16), cots=((base3, wide), BF16),
        tok2=((n2, narrow), BF16),
        rolled=((n2, narrow), BF16), packed=((n2, 3 * narrow), BF16), mixed=((n2, narrow), BF16),
        joined=((base3, 4 * narrow), BF16), mnorm=((base3, 4 * narrow), BF16),
        merged=((base3, wide), BF16), merged3=((n3, wide), BF16), rolled3=((n3, wide), BF16),
        dproj3=((n3, wide), BF16),
        packed3=((n3, 3 * wide), BF16), mixed3=((n3, wide), BF16),
        dpacked3=((n3, 3 * wide), BF16), dsec=((quads, narrow), BF16),
        dsec2=((n2, narrow), BF16), dpacked=((n2, 3 * narrow), BF16),
    )
    kept = (n2 // SLOT * (narrow // LANES), PACK * SLOT, SLOT)
    ints = dict(lc2=(n2, SLOT), lr2=(n2 // SLOT, SLOT), lc3=(n3, SLOT), lr3=(n3 // SLOT, SLOT))
    scratch |= {name: (shape, jnp.int32) for name, shape in ints.items()}
    scratch["kept"] = (kept, F32)
    for name in LATE:
        scratch["v_" + name] = (inputs[name].shape, inputs[name].dtype)
    copies = len(ways) * 3
    for n, way in enumerate(ways):
        width = narrow if way.rows == rows else wide
        if n not in (0, 1, 3):
            scratch[f"row{n}"] = ((way.row, width), BF16)
        scratch[f"col{n}"] = ((way.col, width), BF16)
        for i, size in enumerate(way.sizes()):
            scratch[f"h{n}_{i}"] = ((size, width), BF16)
    for name, shape in (("g3", (m3, 4 * wide)), ("gm", (mm, wide)), ("g2", (m2, 4 * narrow))):
        scratch[name] = ((2, chips, nr) + shape, BF16)
        for i, lead in enumerate(
            ((chips, nr), (chips, nr), (max(chips - 1, 1), nr), (nr,), (max(nr - 1, 1),))
        ):
            scratch[f"{name}_{i}"] = (lead + shape, BF16)
        copies += chips + (chips - 1) * nr + nr - 1
    for i, lead in enumerate(((), (), (), (max(chips - 1, 1),), (), (max(nr - 1, 1),))):
        scratch[f"gg_{i}"] = (lead + (1, gains), F32)
    copies += chips + nr - 1
    spaces = [pltpu.VMEM(s, d) for s, d in scratch.values()]
    spaces += [pltpu.SemaphoreType.DMA((n,)) for n in (copies, copies, len(LATE))]
    results = pl.pallas_call(
        functools.partial(
            whole_kernel, {k: len(v) for k, v in codes.items()}, list(inputs), list(outs), list(scratch) + ["send", "recv", "loaded"]
        ),
        out_shape=[jax.ShapeDtypeStruct(s, d) for s, d in outs.values()],
        in_specs=[
            pl.BlockSpec(
                memory_space=pltpu.SMEM if name == "shifts" else pl.ANY if name in LATE else pltpu.VMEM
            )
            for name in inputs
        ],
        out_specs=[pl.BlockSpec(memory_space=pltpu.VMEM)] * len(outs),
        scratch_shapes=spaces,
        compiler_params=pltpu.CompilerParams(
            collective_id=0, has_side_effects=True, vmem_limit_bytes=60 * 2**20
        ),
        name="block",
    )(*inputs.values())
    flats = [
        (m * width // LANES, LANES)
        for m, width in (
            (m2, 3 * narrow), (m2, narrow), (mm, wide), (m3, 3 * wide), (m3, wide)
        )
    ]
    final = pl.pallas_call(
        finish_kernel,
        out_shape=[
            jax.ShapeDtypeStruct(cotangent.shape, BF16),
            jax.ShapeDtypeStruct(tokens.shape, BF16),
            jax.ShapeDtypeStruct((gains // LANES, LANES), F32),
        ]
        + [jax.ShapeDtypeStruct(shape, BF16) for shape in flats],
        scratch_shapes=[pltpu.VMEM(shape, F32) for shape in flats],
        name="finish",
    )(*results)
    return tuple(final[:2]) + tuple(x.reshape(-1) for x in final[2:])


def solution(mesh):
    tile = P(("groups", "rows"), "cols", None)
    spread = P(("groups", "rows", "cols"))
    return jax.shard_map(
        on_device,
        mesh=mesh,
        in_specs=(tile, tile) + (P(),) * 9,
        out_specs=(tile, tile, P("groups")) + (spread,) * 5,
        check_vma=False,
    )
```
